128 devices in a mesh: ctx: 32 (over z, y_lo, x), grp: 4 (over y_hi, core).
Axes of the slice: x: 4, y: 4 (y_hi: 2, y_lo: 2; y = y_hi * 2 + y_lo), z: 4, core: 2. Of those that a mesh axis runs over, the one named last changes fastest.
Arguments:
- query_input: bfloat16 [16384, 4096], P(('ctx', 'grp')), may hold values from -6 to 6
- key_input: bfloat16 [16384, 4096], P(('ctx', 'grp')), may hold values from -6 to 6
- value_input: bfloat16 [16384, 4096], P(('ctx', 'grp')), may hold values from -6 to 6
- out_grad: bfloat16 [16384, 4096], P(('ctx', 'grp')), may hold values from -6 to 6
- residues: float32 [8, 16], replicated, may hold values from -2 to 2
- decay_rates: float32 [8, 16], replicated, may hold values from 3.0517578e-06 to 0.15
Outputs:
- output: float32 [16384, 4096], P(('ctx', 'grp'))
- query_grad: float32 [16384, 4096], P(('ctx', 'grp'))
- key_grad: float32 [16384, 4096], P(('ctx', 'grp'))
- value_grad: float32 [16384, 4096], P(('ctx', 'grp'))
- residue_grad: float32 [8, 16], replicated
The draws below stay inside these ranges and needn't reach their ends.
All inputs are finite; a program needn't handle non-finite values.
Results may differ from the reference program's by a relative error of at most 0.0055.
Values may be sent and summed in bfloat16 or wider, within the bound.
A program may use at most 192 MiB of HBM per device.

```python
import math
import jax
import jax.numpy as jnp
from jax import lax

D = 4096
GROUP = 512
MODES = 16
TOK_DEV = 512
SEQ = 16384
GROUPS = 8


def pair_law(key):
    shape = (GROUPS, MODES // 2)
    pick = jax.random.uniform(jax.random.fold_in(key, 11), shape)
    level = jax.random.uniform(jax.random.fold_in(key, 12), shape)
    spread = jax.random.uniform(jax.random.fold_in(key, 13), shape)
    slow_lo = jnp.log(0.07 / SEQ)
    slow_hi = jnp.log(1.7 / SEQ)
    mid_lo = jnp.log(jnp.minimum(0.15 / TOK_DEV, 0.02))
    mid_hi = jnp.log(jnp.minimum(0.6 / TOK_DEV, 0.08))
    fast_hi = jnp.log(0.11)
    slower = pick < 0.3
    middle = jnp.logical_and(pick >= 0.3, pick < 0.7)
    fast_logs = mid_hi + level * (fast_hi - mid_hi)
    mid_logs = mid_lo + level * (mid_hi - mid_lo)
    slow_logs = slow_lo + level * (slow_hi - slow_lo)
    logs = jnp.where(slower, slow_logs, jnp.where(middle, mid_logs, fast_logs))
    base = jnp.exp(logs)
    ratio = jnp.exp(jnp.log(1.1) + spread * (jnp.log(1.25) - jnp.log(1.1)))
    return (base.astype(jnp.float32), ratio.astype(jnp.float32))


def draw_decay_rates(key, part):
    base, ratio = pair_law(key)
    rates = jnp.stack([base, base * ratio], axis=2)
    return rates.reshape(GROUPS, MODES).astype(jnp.float32)


def draw_residues(key, part):
    base, ratio = pair_law(key)
    shape = (GROUPS, MODES // 2)
    sign_draw = jax.random.uniform(jax.random.fold_in(key, 21), shape)
    signs = jnp.where(sign_draw < 0.5, -1.0, 1.0)
    size_draw = jax.random.uniform(jax.random.fold_in(key, 22), shape)
    magnitude = 0.7 + 0.6 * size_draw
    balance = 0.88 + 0.08 * jax.random.uniform(jax.random.fold_in(key, 23), shape)
    leading = signs * magnitude * 3.5 * jnp.sqrt(base)
    values = jnp.stack([leading, -balance * leading], axis=2)
    return values.reshape(GROUPS, MODES).astype(jnp.float32)


def level_of(key, shape, split, smallest, largest):
    loudness = 1.0
    for position, parts in split:
        draws = jax.random.uniform(jax.random.fold_in(jax.random.fold_in(key, 6), position), (parts,), jnp.float32, smallest / len(split), largest / len(split))
        loudness = loudness * jnp.repeat(jnp.exp(draws), shape[position] // parts).reshape((-1,) + (1,) * (len(shape) - 1 - position))
    return loudness


def normal_values(rng, extent, scale, bound, split=(), dtype=jnp.bfloat16):
    array = jax.random.normal(rng, extent, jnp.float32) * scale
    if len(split) > 0:
        array = level_of(rng, extent, split, -0.22, 0.18) * array
    return jnp.clip(array, min=-bound, max=bound).astype(dtype)


def setup_inputs(seed: int = 0) -> dict:
    streams_of = jax.random.split(jax.random.key(seed), 7)
    return {
        "query_input": normal_values(streams_of[0], (SEQ, D), 1.0, 6.0, ((0, 128),)),
        "key_input": normal_values(streams_of[1], (SEQ, D), 1.0, 6.0, ((0, 128),)),
        "value_input": normal_values(streams_of[2], (SEQ, D), 1.0, 6.0, ((0, 128),)),
        "out_grad": normal_values(streams_of[3], (SEQ, D), 1.0, 6.0, ((0, 128),)),
        "residues": draw_residues(jax.random.fold_in(streams_of[6], 71), 0),
        "decay_rates": draw_decay_rates(jax.random.fold_in(streams_of[6], 71), 0),
    }


def causal_conv(filter_row, signal):
    length = signal.shape[0]
    total = 2 * length
    spectrum_filter = jnp.fft.rfft(filter_row.astype(jnp.float32), n=total)
    spectrum_signal = jnp.fft.rfft(signal.astype(jnp.float32), n=total, axis=0)
    result = jnp.fft.irfft(spectrum_filter[:, None] * spectrum_signal, n=total, axis=0)
    return result[:length].astype(jnp.float32)

def reference(query_input, key_input, value_input, out_grad, residues, decay_rates):
    length = query_input.shape[0]
    groups = residues.shape[0]
    lags = jnp.arange(length).astype(jnp.float32)
    kernel = jnp.exp(-decay_rates[:, :, None] * lags[None, None, :])
    filters = lax.optimization_barrier(jnp.sum(residues[:, :, None] * kernel, axis=1))
    product = (key_input.astype(jnp.float32) * value_input.astype(jnp.float32)).astype(jnp.bfloat16)
    inner_grad = (out_grad.astype(jnp.float32) * query_input.astype(jnp.float32)).astype(jnp.bfloat16)
    prod_groups = product.reshape(length, groups, GROUP).transpose(1, 0, 2)
    grad_groups = inner_grad.reshape(length, groups, GROUP).transpose(1, 0, 2)

    def per_group(items):
        filter_row, kernel_rows, signal, grad_signal = items
        mixed = causal_conv(filter_row, signal)
        conv_grad = jnp.flip(causal_conv(filter_row, jnp.flip(grad_signal, 0)), 0)
        total = 2 * length
        spec_prod = jnp.fft.rfft(signal.astype(jnp.float32), n=total, axis=0)
        spec_grad = jnp.fft.rfft(grad_signal.astype(jnp.float32), n=total, axis=0)
        cross = jnp.fft.irfft(lax.optimization_barrier(jnp.sum(jnp.conj(spec_prod) * spec_grad, axis=1)), n=total)
        cross = cross[:length].astype(jnp.float32)
        residue_row = lax.optimization_barrier(jnp.sum(kernel_rows * cross[None, :], axis=1))
        return (mixed, conv_grad, residue_row)
    mixed, conv_grad, residue_sum = lax.map(per_group, (filters, kernel, prod_groups, grad_groups))
    width = groups * GROUP
    mixed = mixed.transpose(1, 0, 2).reshape(length, width)
    conv_grad = conv_grad.transpose(1, 0, 2).reshape(length, width)
    output = query_input.astype(jnp.float32) * mixed
    query_grad = out_grad.astype(jnp.float32) * mixed
    key_grad = conv_grad * value_input.astype(jnp.float32)
    value_grad = conv_grad * key_input.astype(jnp.float32)
    residue_grad = residue_sum / (length * math.sqrt(GROUP))
    return (output, query_grad, key_grad, value_grad, residue_grad)
```

```python
import math

import jax
import jax.numpy as jnp
from jax import lax
from jax.experimental import pallas as pl
from jax.experimental.pallas import tpu as pltpu
from jax.sharding import PartitionSpec as P

GROUP = 512
MODES = 16
LANES = 128
MESH = pl.DeviceIdType.MESH


def iota(shape, axis):
    return lax.broadcasted_iota(jnp.int32, shape, axis)


def split(x):
    hi = x.astype(jnp.bfloat16)
    lo = (x - hi.astype(jnp.float32)).astype(jnp.bfloat16)
    return hi, lo


def column(row):
    eye = iota((MODES, MODES), 0) == iota((MODES, MODES), 1)
    return jnp.sum(jnp.where(eye, jnp.broadcast_to(row, (MODES, MODES)), 0.0), axis=1, keepdims=True)


def gated(a, b):
    return (a.astype(jnp.float32) * b.astype(jnp.float32)).astype(jnp.bfloat16)


def exchange_kernel(
    count, groups, span, inner,
    q_hbm, k_hbm, v_hbm, o_hbm, decay_ref,
    state_ref, total_ref,
    ins, prod, grad, send, recv, back, acol, vbuf, v_one, v_two, v_three,
    load_sem, sems,
):
    me = lax.axis_index("ctx") * inner + lax.axis_index("grp")

    def place(j):
        return (lax.div(j, inner), lax.rem(j, inner))

    sources = (q_hbm, k_hbm, v_hbm, o_hbm)

    def load(g, n):
        return pltpu.make_async_copy(
            sources[n].at[:, pl.ds(pl.multiple_of(g * GROUP, GROUP), GROUP)],
            ins.at[n, g],
            load_sem.at[g, n],
        )

    for g in range(groups):
        for n in range(4):
            load(g, n).start()

    barrier = pltpu.get_barrier_semaphore()

    def greet(d, c):
        pl.semaphore_signal(
            barrier, inc=1, device_id=place(lax.rem(me + d, count)), device_id_type=MESH
        )
        return c

    lax.fori_loop(1, count, greet, 0)

    lane = iota((MODES, LANES), 1).astype(jnp.float32)

    for g in range(groups):
        rates = jnp.broadcast_to(column(decay_ref[g : g + 1, :]), (MODES, LANES))
        acol[g * MODES : (g + 1) * MODES, :] = rates

    def states(g, c):
        for n in range(4):
            load(g, n).wait()
        p = gated(ins[1, g], ins[2, g])
        r = gated(ins[3, g], ins[0, g])
        prod[g] = p
        grad[g] = r
        rates = acol[pl.ds(pl.multiple_of(g * MODES, MODES), MODES), :]
        to_end = jnp.concatenate(split(jnp.exp(-rates * (span - 1.0 - lane))), axis=0)
        from_start = jnp.concatenate(split(jnp.exp(-rates * lane)), axis=0)
        ends = jnp.dot(to_end, p, preferred_element_type=jnp.float32)
        starts = jnp.dot(from_start, r, preferred_element_type=jnp.float32)
        ends = ends[:MODES] + ends[MODES:]
        starts = starts[:MODES] + starts[MODES:]
        for k in range(4):
            send[pl.ds(g * 128 + k, MODES, stride=8), :] = ends[:, k * LANES : (k + 1) * LANES]
            send[pl.ds(g * 128 + 4 + k, MODES, stride=8), :] = starts[:, k * LANES : (k + 1) * LANES]
        return c

    lax.fori_loop(0, groups, states, 0)

    def tile(ref, j):
        return ref.at[pl.ds(pl.multiple_of(j * 8, 8), 8), :]

    def scatter(source, target, send_sem, recv_sem):
        def one(d, c):
            j = lax.rem(me + d, count)
            pltpu.make_async_remote_copy(
                src_ref=tile(source, j),
                dst_ref=tile(target, me),
                send_sem=send_sem,
                recv_sem=recv_sem,
                device_id=place(j),
                device_id_type=MESH,
            ).start()
            return c

        lax.fori_loop(1, count, one, 0)

    def await_all(ref, sem):
        part = ref.at[pl.ds(0, (count - 1) * 8), :]
        pltpu.make_async_copy(part, part, sem).wait()

    pl.semaphore_wait(barrier, count - 1)
    scatter(send, recv, sems.at[0], sems.at[1])

    row = iota((span, LANES), 0)
    col = iota((span, LANES), 1)
    flip = (row + col == span - 1).astype(jnp.bfloat16)
    here = iota((MODES, LANES), 1) - iota((MODES, LANES), 0)

    def pairs(g, total):
        pair = lax.dot_general(
            prod[g], grad[g], (((1,), (1,)), ((), ())), preferred_element_type=jnp.float32
        )
        hi, lo = split(pair)
        turned = jnp.dot(hi, flip, preferred_element_type=jnp.float32) + jnp.dot(
            lo, flip, preferred_element_type=jnp.float32
        )
        lagged = pltpu.roll(turned, 0, 1, stride=1, stride_axis=0)
        cross = jnp.sum(jnp.where(col >= row, lagged, 0.0), axis=0, keepdims=True)
        rates = acol[pl.ds(pl.multiple_of(g * MODES, MODES), MODES), :]
        inside = jnp.sum(jnp.exp(-rates * (span - 1.0 - lane)) * cross, axis=1, keepdims=True)
        return total + jnp.sum(jnp.where(here == g * MODES, inside, 0.0), axis=0, keepdims=True)

    share = lax.fori_loop(0, groups, pairs, jnp.zeros((1, LANES), jnp.float32))

    mine = pl.ds(pl.multiple_of(me * 8, 8), 8)
    await_all(recv, sems.at[1])
    recv[mine, :] = send[mine, :]

    rate = jnp.broadcast_to(acol[pl.ds(me, 1), :], (4, LANES))
    factor = jnp.exp(-rate * float(span))
    zero = jnp.zeros((4, LANES), jnp.float32)

    def step(i, carry):
        rising, falling, acc = carry
        up = pl.multiple_of(i * 8, 8)
        down = pl.multiple_of((count - 1 - i) * 8, 8)
        back[pl.ds(up, 4), :] = rising
        back[pl.ds(down + 4, 4), :] = falling
        acc = acc + rising * recv[pl.ds(up + 4, 4), :]
        rising = factor * rising + recv[pl.ds(up, 4), :]
        falling = factor * falling + recv[pl.ds(down + 4, 4), :]
        return rising, falling, acc

    rising, falling, acc = lax.fori_loop(0, count, step, (zero, zero, zero), unroll=8)
    total = jnp.sum(jnp.sum(jnp.exp(-rate) * acc, axis=0, keepdims=True), axis=1, keepdims=True)
    mode = iota((1, LANES), 1) == me
    share = share + jnp.where(mode, jnp.broadcast_to(total, (1, LANES)), 0.0)

    def reduce(buf, radix, stride, value, sem, out_sem, work=None):
        digit = lax.rem(lax.div(me, stride), radix)
        base = me - digit * stride
        vbuf[sem // 2] = value
        copies = []
        for d in range(1, radix):
            other = lax.rem(digit + d, radix)
            copy = pltpu.make_async_remote_copy(
                src_ref=vbuf.at[sem // 2],
                dst_ref=buf.at[digit],
                send_sem=sems.at[sem],
                recv_sem=sems.at[out_sem],
                device_id=place(base + other * stride),
                device_id_type=MESH,
            )
            copy.start()
        if work is not None:
            work()
        part = buf.at[pl.ds(0, radix - 1)]
        pltpu.make_async_copy(part, part, sems.at[out_sem]).wait()
        buf[digit] = value
        summed = jnp.sum(buf[...], axis=0)
        pltpu.make_async_copy(part, part, sems.at[sem]).wait()
        return summed

    def phase_two():
        scatter(back, state_ref, sems.at[2], sems.at[3])
        state_ref[mine, :] = back[mine, :]

    share = reduce(v_one, 4, 1, share, 4, 5, phase_two)
    share = reduce(v_two, 8, 4, share, 6, 7)
    share = reduce(v_three, 4, 32, share, 8, 9)
    total_ref[...] = share
    await_all(send, sems.at[0])
    await_all(back, sems.at[2])
    await_all(state_ref, sems.at[3])


def exchange(query_input, key_input, value_input, out_grad, decays):
    inner = lax.axis_size("grp")
    count = lax.axis_size("ctx") * inner
    span, width = query_input.shape
    groups = width // GROUP
    rows = count * 8
    f32 = jnp.float32
    bf16 = jnp.bfloat16

    def body(*refs):
        exchange_kernel(count, groups, span, inner, *refs)

    hbm = pl.BlockSpec(memory_space=pl.ANY)
    vmem = pl.BlockSpec(memory_space=pltpu.VMEM)
    return pl.pallas_call(
        body,
        out_shape=(
            jax.ShapeDtypeStruct((rows, LANES), f32),
            jax.ShapeDtypeStruct((1, LANES), f32),
        ),
        in_specs=[hbm] * 4 + [vmem],
        out_specs=(vmem, vmem),
        scratch_shapes=[
            pltpu.VMEM((4, groups, span, GROUP), bf16),
            pltpu.VMEM((groups, span, GROUP), bf16),
            pltpu.VMEM((groups, span, GROUP), bf16),
            pltpu.VMEM((rows, LANES), f32),
            pltpu.VMEM((rows, LANES), f32),
            pltpu.VMEM((rows, LANES), f32),
            pltpu.VMEM((groups * MODES, LANES), f32),
            pltpu.VMEM((5, 1, LANES), f32),
            pltpu.VMEM((4, 1, LANES), f32),
            pltpu.VMEM((8, 1, LANES), f32),
            pltpu.VMEM((4, 1, LANES), f32),
            pltpu.SemaphoreType.DMA((groups, 4)),
            pltpu.SemaphoreType.DMA((10,)),
        ],
        compiler_params=pltpu.CompilerParams(
            collective_id=0, has_side_effects=True, vmem_limit_bytes=40 * 1024 * 1024
        ),
    )(query_input, key_input, value_input, out_grad, decays)


def finish_kernel(
    span, scale,
    q_ref, k_ref, v_ref, o_ref, state_ref, total_ref, res_ref, decay_ref,
    out_ref, qg_ref, kg_ref, vg_ref, rg_ref,
):
    g = pl.program_id(0)
    q, k, v, o = (ref[...].astype(jnp.float32) for ref in (q_ref, k_ref, v_ref, o_ref))
    p = (k * v).astype(jnp.bfloat16)
    r = (o * q).astype(jnp.bfloat16)
    decay_row = decay_ref[pl.ds(g, 1), :]
    res_row = res_ref[pl.ds(g, 1), :]
    rates = column(decay_row)
    weights = column(res_row)
    lane_i = iota((MODES, LANES), 1)
    lane = lane_i.astype(jnp.float32)
    turned = jnp.where(lane_i == 0, 0, LANES - lane_i).astype(jnp.float32)
    row = iota((span, LANES), 0)
    col = iota((span, LANES), 1)

    def toeplitz(lags, keep):
        line = jnp.sum(weights * jnp.exp(-rates * lags), axis=0, keepdims=True)
        full = pltpu.roll(jnp.broadcast_to(line, (span, LANES)), 0, 1, stride=1, stride_axis=0)
        return split(jnp.where(keep, full, 0.0))

    down_hi, down_lo = toeplitz(turned, row >= col)
    up_hi, up_lo = toeplitz(lane, row <= col)

    def dot(a, b):
        return jnp.dot(a, b, preferred_element_type=jnp.float32)

    token = iota((span, MODES), 0).astype(jnp.float32)
    rise = split(res_row * jnp.exp(-decay_row * (token + 1.0)))
    fall = split(res_row * jnp.exp(-decay_row * (span - token)))

    def carried(table, first):
        state = jnp.concatenate(
            [state_ref[pl.ds(first + n, MODES, stride=8), :] for n in range(4)], axis=1
        )
        hi, lo = split(state)
        return dot(table[0], hi) + dot(table[0], lo) + dot(table[1], hi)

    mixed = dot(down_hi, p) + dot(down_lo, p) + carried(rise, 0)
    out_ref[...] = q * mixed
    qg_ref[...] = o * mixed
    conv = dot(up_hi, r) + dot(up_lo, r) + carried(fall, 4)
    kg_ref[...] = conv * v
    vg_ref[...] = conv * k

    @pl.when(g == 0)
    def _():
        groups = rg_ref.shape[0]
        spread = jnp.broadcast_to(total_ref[...], (groups, LANES))
        own = lax.div(iota((groups, LANES), 1), MODES) == iota((groups, LANES), 0)
        spread = jnp.where(own, spread, 0.0)
        out = spread
        for n in range(1, groups):
            out = out + pltpu.roll(spread, LANES - n * MODES, 1)
        rg_ref[...] = out[:, :MODES] * scale


def finish(query_input, key_input, value_input, out_grad, state, total, residues, decays, length):
    span, width = query_input.shape
    groups = width // GROUP
    scale = 1.0 / (length * math.sqrt(GROUP))

    def body(*refs):
        finish_kernel(span, scale, *refs)

    block = pl.BlockSpec((span, GROUP), lambda g: (0, g))
    small = pl.BlockSpec(residues.shape, lambda g: (0, 0))
    big = jax.ShapeDtypeStruct((span, width), jnp.float32)
    return pl.pallas_call(
        body,
        grid=(groups,),
        out_shape=(big, big, big, big, jax.ShapeDtypeStruct(residues.shape, jnp.float32)),
        in_specs=[block] * 4
        + [
            pl.BlockSpec((MODES * 8, LANES), lambda g: (g, 0)),
            pl.BlockSpec((1, LANES), lambda g: (0, 0)),
            small,
            small,
        ],
        out_specs=(block, block, block, block, small),
        compiler_params=pltpu.CompilerParams(
            dimension_semantics=("arbitrary",), vmem_limit_bytes=40 * 1024 * 1024
        ),
    )(query_input, key_input, value_input, out_grad, state, total, residues, decays)


def on_device(query_input, key_input, value_input, out_grad, residues, decay_rates):
    length = query_input.shape[0] * lax.axis_size("ctx") * lax.axis_size("grp")
    state, total = exchange(query_input, key_input, value_input, out_grad, decay_rates)
    return finish(
        query_input, key_input, value_input, out_grad, state, total, residues, decay_rates, length
    )


def solution(mesh):
    rows = P(("ctx", "grp"), None)
    return jax.shard_map(
        on_device,
        mesh=mesh,
        in_specs=(rows, rows, rows, rows, P(), P()),
        out_specs=(rows, rows, rows, rows, P()),
        check_vma=False,
    )
```

```python
import math

import jax
import jax.numpy as jnp
from jax import lax
from jax.experimental import pallas as pl
from jax.experimental.pallas import tpu as pltpu
from jax.sharding import PartitionSpec as P

GROUP = 512
MODES = 16
LANES = 128
TILE = 8
QUARTERS = GROUP // LANES
MESH = pl.DeviceIdType.MESH
MIB = 1024 * 1024


def iota(shape, axis):
    return lax.broadcasted_iota(jnp.int32, shape, axis)


def split(x):
    hi = x.astype(jnp.bfloat16)
    lo = (x - hi.astype(jnp.float32)).astype(jnp.bfloat16)
    return hi, lo


def dot(a, b):
    return jnp.dot(a, b, preferred_element_type=jnp.float32)


def column(row):
    eye = iota((MODES, MODES), 0) == iota((MODES, MODES), 1)
    return jnp.sum(jnp.where(eye, jnp.broadcast_to(row, (MODES, MODES)), 0.0), axis=1, keepdims=True)


def gated(a, b):
    return (a.astype(jnp.float32) * b.astype(jnp.float32)).astype(jnp.bfloat16)


def exchange_kernel(
    count, groups, span, inner,
    q_hbm, k_hbm, v_hbm, o_hbm, res_hbm, decay_hbm,
    state_ref, total_ref, ins, mixed_ref, conv_ref, rise_ref, fall_ref,
    prod, grad, send, theirs, comb, recv, back, half, sib, acol, xs, small,
    vbuf, v_one, v_two, v_three,
    load_sem, small_sem, swap_sem, sems,
):
    me = lax.axis_index("ctx") * inner + lax.axis_index("grp")
    chips = count // 2
    chip = lax.div(me, 2)
    core = lax.rem(me, 2)
    sibling = me + 1 - 2 * core
    part_groups = groups // 2
    part_rows = part_groups * MODES
    first = core * part_groups
    other = part_groups - first

    def place(j):
        return (lax.div(j, inner), lax.rem(j, inner))

    sources = (q_hbm, k_hbm, v_hbm, o_hbm)

    def load(g, n):
        return pltpu.make_async_copy(
            sources[n].at[:, pl.ds(pl.multiple_of(g * GROUP, GROUP), GROUP)],
            ins.at[n, g],
            load_sem.at[g, n],
        )

    tables = [
        pltpu.make_async_copy(decay_hbm, small.at[0], small_sem.at[0]),
        pltpu.make_async_copy(res_hbm, small.at[1], small_sem.at[1]),
    ]
    for copy in tables:
        copy.start()

    def ordered(s):
        return jnp.where(s < part_groups, other + s, first + s - part_groups)

    for s in range(groups):
        for n in range(4):
            load(ordered(s), n).start()

    barrier = pltpu.get_barrier_semaphore()
    pl.semaphore_signal(barrier, inc=1, device_id=place(sibling), device_id_type=MESH)

    def peer(d):
        return lax.rem(chip + d, chips)

    def greet(d, c):
        pl.semaphore_signal(
            barrier, inc=1, device_id=place(peer(d) * 2 + core), device_id_type=MESH
        )
        return c

    lax.fori_loop(1, chips, greet, 0)

    lane_i = iota((MODES, LANES), 1)
    lane = lane_i.astype(jnp.float32)
    for copy in tables:
        copy.wait()
    for g in range(groups):
        rates = jnp.broadcast_to(column(small[0, g : g + 1, :]), (MODES, LANES))
        acol[g * MODES : (g + 1) * MODES, :] = rates

    def group_rates(g):
        return acol[pl.ds(pl.multiple_of(g * MODES, MODES), MODES), :]

    block = MODES * TILE

    def swap_copy(source, target, n, where, phase):
        return pltpu.make_async_remote_copy(
            src_ref=source.at[pl.ds(pl.multiple_of(where, block), block), :],
            dst_ref=target.at[pl.ds(n * block, block), :],
            send_sem=swap_sem.at[phase, 0, n],
            recv_sem=swap_sem.at[phase, 1, n],
            device_id=place(sibling),
            device_id_type=MESH,
        )

    def out_copy(n):
        return swap_copy(send, theirs, n, (other + n) * block, 0)

    def states(s, c):
        g = ordered(s)
        for n in range(4):
            load(g, n).wait()
        p = gated(ins[1, g], ins[2, g])
        r = gated(ins[3, g], ins[0, g])
        prod[g] = p
        grad[g] = r
        rates = group_rates(g)
        to_end = jnp.concatenate(split(jnp.exp(-rates * (span - 1.0 - lane))), axis=0)
        from_start = jnp.concatenate(split(jnp.exp(-rates * lane)), axis=0)
        ends = dot(to_end, p)
        starts = dot(from_start, r)
        ends = ends[:MODES] + ends[MODES:]
        starts = starts[:MODES] + starts[MODES:]
        for k in range(QUARTERS):
            cut = slice(k * LANES, (k + 1) * LANES)
            send[pl.ds(g * block + k, MODES, stride=TILE), :] = ends[:, cut]
            send[pl.ds(g * block + QUARTERS + k, MODES, stride=TILE), :] = starts[:, cut]
        return c

    lax.fori_loop(0, part_groups, states, 0)
    pl.semaphore_wait(barrier, chips)
    for n in range(part_groups):
        out_copy(n).start()
    lax.fori_loop(part_groups, groups, states, 0)

    sub = iota((TILE, LANES), 0)
    lead = (sub < QUARTERS) == (core == 0)

    def row_factor(n, width):
        rate = acol[pl.ds(first * MODES + n, 1), :]
        return jnp.broadcast_to(jnp.exp(-rate * float(span)), (width, LANES))

    def tile_at(n):
        return pl.ds(pl.multiple_of(n * TILE, TILE), TILE)

    def own_tile(n):
        return pl.ds(pl.multiple_of(first * block + n * TILE, TILE), TILE)

    def combine(n, c):
        factor = row_factor(n, TILE)
        mine = send[own_tile(n), :]
        got = theirs[tile_at(n), :]
        comb[tile_at(n), :] = jnp.where(lead, factor, 1.0) * mine + jnp.where(lead, 1.0, factor) * got
        return c

    for n in range(part_groups):
        out_copy(n).wait_recv()
        lax.fori_loop(n * MODES, (n + 1) * MODES, combine, 0, unroll=8)

    def scatter(source, target, send_sem, recv_sem):
        def one(d, c):
            t = peer(d)
            pltpu.make_async_remote_copy(
                src_ref=source.at[tile_at(t), :],
                dst_ref=target.at[tile_at(chip), :],
                send_sem=send_sem,
                recv_sem=recv_sem,
                device_id=place(t * 2 + core),
                device_id_type=MESH,
            ).start()
            return c

        lax.fori_loop(1, chips, one, 0)

    def await_all(ref, sem):
        part = ref.at[pl.ds(0, (chips - 1) * TILE), :]
        pltpu.make_async_copy(part, part, sem).wait()

    scatter(comb, recv, sems.at[0], sems.at[1])

    row = iota((span, LANES), 0)
    col = iota((span, LANES), 1)
    flip = (row + col == span - 1).astype(jnp.bfloat16)
    here = lane_i - iota((MODES, LANES), 0)

    xs[...] = jnp.zeros_like(xs)

    def within_chip(n, c):
        base = pl.multiple_of(first * block + n * TILE, TILE)
        near = pl.multiple_of(n * TILE, TILE)
        early = jnp.where(
            core == 0,
            send[pl.ds(base, QUARTERS), :] * theirs[pl.ds(near + QUARTERS, QUARTERS), :],
            theirs[pl.ds(near, QUARTERS), :] * send[pl.ds(base + QUARTERS, QUARTERS), :],
        )
        xs[pl.ds(first * MODES + n, 1), :] = jnp.sum(early, axis=0, keepdims=True)
        return c

    lax.fori_loop(0, part_rows, within_chip, 0, unroll=8)

    def pairs(g, total):
        pair = lax.dot_general(
            prod[g], grad[g], (((1,), (1,)), ((), ())), preferred_element_type=jnp.float32
        )
        hi, lo = split(pair)
        turned = dot(hi, flip) + dot(lo, flip)
        lagged = pltpu.roll(turned, 0, 1, stride=1, stride_axis=0)
        cross = jnp.sum(jnp.where(col >= row, lagged, 0.0), axis=0, keepdims=True)
        rates = group_rates(g)
        chip_part = xs[pl.ds(pl.multiple_of(g * MODES, MODES), MODES), :]
        inside = jnp.exp(-rates * (span - 1.0 - lane)) * cross + jnp.exp(-rates) * chip_part
        inside = jnp.sum(inside, axis=1, keepdims=True)
        return total + jnp.sum(jnp.where(here == g * MODES, inside, 0.0), axis=0, keepdims=True)

    share = lax.fori_loop(0, groups, pairs, jnp.zeros((1, LANES), jnp.float32))

    turned_lags = jnp.where(lane_i == 0, 0, LANES - lane_i).astype(jnp.float32)
    triple = 3 * MODES
    token = iota((span, triple), 0).astype(jnp.float32)
    which = iota((span, triple), 1)

    def local(g, c):
        rates = group_rates(g)
        decay_row = small[0, pl.ds(g, 1), :]
        res_row = small[1, pl.ds(g, 1), :]
        weights = column(res_row)

        def toeplitz(lags, keep):
            line = jnp.sum(weights * jnp.exp(-rates * lags), axis=0, keepdims=True)
            full = pltpu.roll(jnp.broadcast_to(line, (span, LANES)), 0, 1, stride=1, stride_axis=0)
            return jnp.concatenate(split(jnp.where(keep, full, 0.0)), axis=1)

        p = prod[g]
        r = grad[g]
        mixed_ref[g] = dot(toeplitz(turned_lags, row >= col), jnp.concatenate([p, p], axis=0))
        conv_ref[g] = dot(toeplitz(lane, row <= col), jnp.concatenate([r, r], axis=0))
        decay_rows = jnp.concatenate([decay_row] * 3, axis=1)
        res_rows = jnp.concatenate([res_row] * 3, axis=1)

        def table(distance):
            hi, lo = split(res_rows * jnp.exp(-decay_rows * distance))
            return jnp.where(which < 2 * MODES, hi.astype(jnp.float32), lo.astype(jnp.float32)).astype(
                jnp.bfloat16
            )

        rise_ref[g] = table(token + 1.0)
        fall_ref[g] = table(span - token)
        return c

    lax.fori_loop(0, part_groups, local, 0)

    own = tile_at(chip)
    await_all(recv, sems.at[1])
    recv[own, :] = comb[own, :]

    rate = jnp.broadcast_to(acol[pl.ds(first * MODES + chip, 1), :], (QUARTERS, LANES))
    leap = jnp.exp(-rate * (2.0 * span))
    zero = jnp.zeros((QUARTERS, LANES), jnp.float32)

    def step(i, carry):
        rising, falling, acc = carry
        up = pl.multiple_of(i * TILE, TILE)
        down = pl.multiple_of((chips - 1 - i) * TILE, TILE)
        back[pl.ds(up, QUARTERS), :] = rising
        back[pl.ds(down + QUARTERS, QUARTERS), :] = falling
        acc = acc + rising * recv[pl.ds(up + QUARTERS, QUARTERS), :]
        rising = leap * rising + recv[pl.ds(up, QUARTERS), :]
        falling = leap * falling + recv[pl.ds(down + QUARTERS, QUARTERS), :]
        return rising, falling, acc

    rising, falling, acc = lax.fori_loop(0, chips, step, (zero, zero, zero), unroll=8)
    scatter(back, half, sems.at[2], sems.at[3])
    half[own, :] = back[own, :]

    total = jnp.sum(jnp.sum(jnp.exp(-rate) * acc, axis=0, keepdims=True), axis=1, keepdims=True)
    mode = iota((1, LANES), 1) == first * MODES + chip
    share = share + jnp.where(mode, jnp.broadcast_to(total, (1, LANES)), 0.0)

    def reduce(level, buf, radix, stride, value, begin, end):
        digit = lax.rem(lax.div(me, stride), radix)
        base = me - digit * stride
        send_sem = sems.at[4 + 2 * level]
        recv_sem = sems.at[5 + 2 * level]
        vbuf[level] = value
        for d in range(1, radix):
            pltpu.make_async_remote_copy(
                src_ref=vbuf.at[level],
                dst_ref=buf.at[digit],
                send_sem=send_sem,
                recv_sem=recv_sem,
                device_id=place(base + lax.rem(digit + d, radix) * stride),
                device_id_type=MESH,
            ).start()
        lax.fori_loop(begin, end, local, 0)
        part = buf.at[pl.ds(0, radix - 1)]
        pltpu.make_async_copy(part, part, recv_sem).wait()
        buf[digit] = value
        summed = jnp.sum(buf[...], axis=0)
        pltpu.make_async_copy(part, part, send_sem).wait()
        return summed

    share = reduce(0, v_one, 2, 1, share, part_groups, part_groups + 1)
    share = reduce(1, v_two, 8, 2, share, part_groups + 1, groups)
    share = reduce(2, v_three, 8, 16, share, 0, 0)
    total_ref[...] = share

    await_all(half, sems.at[3])

    def back_copy(n):
        return pltpu.make_async_remote_copy(
            src_ref=sib.at[pl.ds(n * block, block), :],
            dst_ref=state_ref.at[pl.ds(pl.multiple_of((first + n) * block, block), block), :],
            send_sem=swap_sem.at[1, 0, n],
            recv_sem=swap_sem.at[1, 1, n],
            device_id=place(sibling),
            device_id_type=MESH,
        )

    def for_sibling(n, c):
        x = half[tile_at(n), :]
        factor = row_factor(n, TILE)
        sib[tile_at(n), :] = jnp.where(lead, factor * x + send[own_tile(n), :], x)
        return c

    def for_me(n, c):
        x = half[tile_at(n), :]
        factor = row_factor(n, TILE)
        state_ref[own_tile(n), :] = jnp.where(lead, x, factor * x + theirs[tile_at(n), :])
        return c

    for n in range(part_groups):
        lax.fori_loop(n * MODES, (n + 1) * MODES, for_sibling, 0, unroll=8)
        back_copy(n).start()
    lax.fori_loop(0, part_rows, for_me, 0, unroll=8)

    for n in range(part_groups):
        out_copy(n).wait_send()
        back_copy(n).wait()
    await_all(comb, sems.at[0])
    await_all(back, sems.at[2])


def exchange(query_input, key_input, value_input, out_grad, residues, decays):
    inner = lax.axis_size("grp")
    count = lax.axis_size("ctx") * inner
    span, width = query_input.shape
    groups = width // GROUP
    rows = groups * MODES * TILE
    chips = count // 2
    f32 = jnp.float32
    bf16 = jnp.bfloat16

    def body(*refs):
        exchange_kernel(count, groups, span, inner, *refs)

    hbm = pl.BlockSpec(memory_space=pltpu.HBM)
    vmem = pl.BlockSpec(memory_space=pltpu.VMEM)
    return pl.pallas_call(
        body,
        out_shape=(
            jax.ShapeDtypeStruct((rows, LANES), f32),
            jax.ShapeDtypeStruct((1, LANES), f32),
            jax.ShapeDtypeStruct((4, groups, span, GROUP), bf16),
            jax.ShapeDtypeStruct((groups, span, GROUP), f32),
            jax.ShapeDtypeStruct((groups, span, GROUP), f32),
            jax.ShapeDtypeStruct((groups, span, 3 * MODES), bf16),
            jax.ShapeDtypeStruct((groups, span, 3 * MODES), bf16),
        ),
        in_specs=[hbm] * 6,
        out_specs=(vmem,) * 7,
        scratch_shapes=[
            pltpu.VMEM((groups, span, GROUP), bf16),
            pltpu.VMEM((groups, span, GROUP), bf16),
            pltpu.VMEM((rows, LANES), f32),
            pltpu.VMEM((rows // 2, LANES), f32),
            pltpu.VMEM((rows // 2, LANES), f32),
            pltpu.VMEM((chips * TILE, LANES), f32),
            pltpu.VMEM((chips * TILE, LANES), f32),
            pltpu.VMEM((rows // 2, LANES), f32),
            pltpu.VMEM((rows // 2, LANES), f32),
            pltpu.VMEM((groups * MODES, LANES), f32),
            pltpu.VMEM((groups * MODES, LANES), f32),
            pltpu.VMEM((2, groups, MODES), f32),
            pltpu.VMEM((3, 1, LANES), f32),
            pltpu.VMEM((2, 1, LANES), f32),
            pltpu.VMEM((8, 1, LANES), f32),
            pltpu.VMEM((8, 1, LANES), f32),
            pltpu.SemaphoreType.DMA((groups, 4)),
            pltpu.SemaphoreType.DMA((2,)),
            pltpu.SemaphoreType.DMA((2, 2, groups // 2)),
            pltpu.SemaphoreType.DMA((10,)),
        ],
        compiler_params=pltpu.CompilerParams(
            collective_id=0, has_side_effects=True, vmem_limit_bytes=20 * MIB
        ),
    )(
        *(
            pltpu.with_memory_space_constraint(a, pltpu.HBM)
            for a in (query_input, key_input, value_input, out_grad, residues, decays)
        )
    )


def finish_kernel(
    groups, scale,
    state_ref, total_ref, ins, mixed_ref, conv_ref, rise_ref, fall_ref,
    out_hbm, qg_hbm, kg_hbm, vg_hbm, rg_ref,
    outs, sems,
):
    targets = (out_hbm, qg_hbm, kg_hbm, vg_hbm)

    def store(g, n):
        return pltpu.make_async_copy(
            outs.at[n, g],
            targets[n].at[:, pl.ds(pl.multiple_of(g * GROUP, GROUP), GROUP)],
            sems.at[n, g],
        )

    def carried(table, g, offset):
        state = jnp.concatenate(
            [
                state_ref[pl.ds(g * MODES * TILE + offset + n, MODES, stride=TILE), :]
                for n in range(QUARTERS)
            ],
            axis=1,
        )
        hi, lo = split(state)
        return dot(table, jnp.concatenate([hi, lo, hi], axis=0))

    def one(g, c):
        mixed = mixed_ref[g] + carried(rise_ref[g], g, 0)
        outs[0, g] = ins[0, g].astype(jnp.float32) * mixed
        store(g, 0).start()
        outs[1, g] = ins[3, g].astype(jnp.float32) * mixed
        store(g, 1).start()
        conv = conv_ref[g] + carried(fall_ref[g], g, QUARTERS)
        outs[2, g] = ins[2, g].astype(jnp.float32) * conv
        store(g, 2).start()
        outs[3, g] = ins[1, g].astype(jnp.float32) * conv
        store(g, 3).start()
        return c

    lax.fori_loop(0, groups, one, 0)

    spread = jnp.broadcast_to(total_ref[...], (groups, LANES))
    own = lax.div(iota((groups, LANES), 1), MODES) == iota((groups, LANES), 0)
    spread = jnp.where(own, spread, 0.0)
    out = spread
    for n in range(1, groups):
        out = out + pltpu.roll(spread, LANES - n * MODES, 1)
    rg_ref[...] = out[:, :MODES] * scale

    for g in range(groups):
        for n in range(4):
            store(g, n).wait()


def finish(parts, span, width, length):
    groups = width // GROUP
    scale = 1.0 / (length * math.sqrt(GROUP))

    def body(*refs):
        finish_kernel(groups, scale, *refs)

    hbm = pl.BlockSpec(memory_space=pltpu.HBM)
    vmem = pl.BlockSpec(memory_space=pltpu.VMEM)
    big = jax.ShapeDtypeStruct((span, width), jnp.float32)
    return pl.pallas_call(
        body,
        out_shape=(big, big, big, big, jax.ShapeDtypeStruct((groups, MODES), jnp.float32)),
        in_specs=[vmem] * 7,
        out_specs=(hbm, hbm, hbm, hbm, vmem),
        scratch_shapes=[
            pltpu.VMEM((4, groups, span, GROUP), jnp.float32),
            pltpu.SemaphoreType.DMA((4, groups)),
        ],
        compiler_params=pltpu.CompilerParams(vmem_limit_bytes=20 * MIB),
    )(*parts)


def on_device(query_input, key_input, value_input, out_grad, residues, decay_rates):
    span, width = query_input.shape
    length = span * lax.axis_size("ctx") * lax.axis_size("grp")
    parts = exchange(query_input, key_input, value_input, out_grad, residues, decay_rates)
    return finish(parts, span, width, length)


def solution(mesh):
    rows = P(("ctx", "grp"), None)
    return jax.shard_map(
        on_device,
        mesh=mesh,
        in_specs=(rows, rows, rows, rows, P(), P()),
        out_specs=(rows, rows, rows, rows, P()),
        check_vma=False,
    )
```

```python
import math

import jax
import jax.numpy as jnp
from jax import lax
from jax.experimental import pallas as pl
from jax.experimental.pallas import tpu as pltpu
from jax.sharding import PartitionSpec as P

GROUP = 512
MODES = 16
LANES = 128
TILE = 8
QUARTERS = GROUP // LANES
RING = 4
EXTRA = TILE + 1
MESH = pl.DeviceIdType.MESH
MIB = 1024 * 1024


def iota(shape, axis):
    return lax.broadcasted_iota(jnp.int32, shape, axis)


def split(x):
    hi = x.astype(jnp.bfloat16)
    lo = (x - hi.astype(jnp.float32)).astype(jnp.bfloat16)
    return hi, lo


def dot(a, b):
    return jnp.dot(a, b, preferred_element_type=jnp.float32)


def column(row):
    eye = iota((MODES, MODES), 0) == iota((MODES, MODES), 1)
    return jnp.sum(jnp.where(eye, jnp.broadcast_to(row, (MODES, MODES)), 0.0), axis=1, keepdims=True)


def gated(a, b):
    return (a.astype(jnp.float32) * b.astype(jnp.float32)).astype(jnp.bfloat16)


def shifts():
    hops = (0, 1, 2, 1)
    every = [(z, y, x) for z in range(RING) for y in range(RING) for x in range(RING)]
    return sorted(every[1:], key=lambda d: -sum(hops[c] for c in d))


def exchange_kernel(
    count, groups, span, inner,
    q_hbm, k_hbm, v_hbm, o_hbm, res_hbm, decay_hbm,
    state_ref, total_ref, ins, mixed_ref, conv_ref, rise_ref, fall_ref,
    prod, grad, send, theirs, comb, recv, back, half, sib, acol, xs, small,
    vbuf, v_one, v_two, v_got,
    load_sem, small_sem, swap_sem, sems,
):
    me = lax.axis_index("ctx") * inner + lax.axis_index("grp")
    chips = count // 2
    chip = lax.div(me, 2)
    core = lax.rem(me, 2)
    sibling = me + 1 - 2 * core
    part_groups = groups // 2
    part_rows = part_groups * MODES
    first = core * part_groups
    other = part_groups - first

    def place(j):
        return (lax.div(j, inner), lax.rem(j, inner))

    sources = (q_hbm, k_hbm, v_hbm, o_hbm)

    def load(g, n):
        return pltpu.make_async_copy(
            sources[n].at[:, pl.ds(pl.multiple_of(g * GROUP, GROUP), GROUP)],
            ins.at[n, g],
            load_sem.at[g, n],
        )

    def ordered(s):
        return jnp.where(s < part_groups, other + s, first + s - part_groups)

    barrier = pltpu.get_barrier_semaphore()
    pl.semaphore_signal(barrier, inc=1, device_id=place(sibling), device_id_type=MESH)

    y_hi = lax.rem(chip, 2)
    x = lax.rem(lax.div(chip, 2), RING)
    y = y_hi * 2 + lax.rem(lax.div(chip, 2 * RING), 2)
    z = lax.div(chip, 4 * RING)

    def peer(d):
        dz, dy, dx = d
        to_z, to_y, to_x = lax.rem(z + dz, RING), lax.rem(y + dy, RING), lax.rem(x + dx, RING)
        return ((to_z * 2 + lax.rem(to_y, 2)) * RING + to_x) * 2 + lax.div(to_y, 2)

    peers = [peer(d) for d in shifts()]
    for t in peers:
        pl.semaphore_signal(
            barrier, inc=1, device_id=place(t * 2 + core), device_id_type=MESH
        )

    tables = [
        pltpu.make_async_copy(decay_hbm, small.at[0], small_sem.at[0]),
        pltpu.make_async_copy(res_hbm, small.at[1], small_sem.at[1]),
    ]
    for copy in tables:
        copy.start()

    for s in range(groups):
        for n in range(4):
            load(ordered(s), n).start()

    lane_i = iota((MODES, LANES), 1)
    lane = lane_i.astype(jnp.float32)
    for copy in tables:
        copy.wait()
    for g in range(groups):
        rates = jnp.broadcast_to(column(small[0, g : g + 1, :]), (MODES, LANES))
        acol[g * MODES : (g + 1) * MODES, :] = rates

    def group_rates(g):
        return acol[pl.ds(pl.multiple_of(g * MODES, MODES), MODES), :]

    block = MODES * TILE

    def swap_copy(source, target, n, where, phase):
        return pltpu.make_async_remote_copy(
            src_ref=source.at[pl.ds(pl.multiple_of(where, block), block), :],
            dst_ref=target.at[pl.ds(n * block, block), :],
            send_sem=swap_sem.at[phase, 0, n],
            recv_sem=swap_sem.at[phase, 1, n],
            device_id=place(sibling),
            device_id_type=MESH,
        )

    def out_copy(n):
        return swap_copy(send, theirs, n, (other + n) * block, 0)

    def states(s, c):
        g = ordered(s)
        for n in range(4):
            load(g, n).wait()
        p = gated(ins[1, g], ins[2, g])
        r = gated(ins[3, g], ins[0, g])
        prod[g] = p
        grad[g] = r
        rates = group_rates(g)
        to_end = jnp.concatenate(split(jnp.exp(-rates * (span - 1.0 - lane))), axis=0)
        from_start = jnp.concatenate(split(jnp.exp(-rates * lane)), axis=0)
        ends = dot(to_end, p)
        starts = dot(from_start, r)
        ends = ends[:MODES] + ends[MODES:]
        starts = starts[:MODES] + starts[MODES:]
        for k in range(QUARTERS):
            cut = slice(k * LANES, (k + 1) * LANES)
            send[pl.ds(g * block + k, MODES, stride=TILE), :] = ends[:, cut]
            send[pl.ds(g * block + QUARTERS + k, MODES, stride=TILE), :] = starts[:, cut]
        return c

    lax.fori_loop(0, part_groups, states, 0)
    pl.semaphore_wait(barrier, chips)
    for n in range(part_groups):
        out_copy(n).start()
    lax.fori_loop(part_groups, groups, states, 0)

    sub = iota((TILE, LANES), 0)
    lead = (sub < QUARTERS) == (core == 0)

    def row_factor(n, width):
        rate = acol[pl.ds(first * MODES + n, 1), :]
        return jnp.broadcast_to(jnp.exp(-rate * float(span)), (width, LANES))

    def tile_at(n):
        return pl.ds(pl.multiple_of(n * TILE, TILE), TILE)

    def own_tile(n):
        return pl.ds(pl.multiple_of(first * block + n * TILE, TILE), TILE)

    def combine(n, c):
        factor = row_factor(n, TILE)
        mine = send[own_tile(n), :]
        got = theirs[tile_at(n), :]
        comb[tile_at(n), :] = jnp.where(lead, factor, 1.0) * mine + jnp.where(lead, 1.0, factor) * got
        return c

    for n in range(part_groups):
        out_copy(n).wait_recv()
        lax.fori_loop(n * MODES, (n + 1) * MODES, combine, 0, unroll=8)

    def scatter(source, target, send_sem, recv_sem):
        for t in peers:
            pltpu.make_async_remote_copy(
                src_ref=source(t),
                dst_ref=target(chip),
                send_sem=send_sem,
                recv_sem=recv_sem,
                device_id=place(t * 2 + core),
                device_id_type=MESH,
            ).start()

    def await_all(part, sem):
        pltpu.make_async_copy(part, part, sem).wait()

    most = pl.ds(0, (chips - 1) * TILE)
    rest = pl.ds(0, chips - 1)
    scatter(lambda t: comb.at[tile_at(t), :], lambda t: recv.at[tile_at(t), :], sems.at[0], sems.at[1])

    row = iota((span, LANES), 0)
    col = iota((span, LANES), 1)
    flip = (row + col == span - 1).astype(jnp.bfloat16)
    here = lane_i - iota((MODES, LANES), 0)

    xs[...] = jnp.zeros_like(xs)

    def within_chip(n, c):
        base = pl.multiple_of(first * block + n * TILE, TILE)
        near = pl.multiple_of(n * TILE, TILE)
        early = jnp.where(
            core == 0,
            send[pl.ds(base, QUARTERS), :] * theirs[pl.ds(near + QUARTERS, QUARTERS), :],
            theirs[pl.ds(near, QUARTERS), :] * send[pl.ds(base + QUARTERS, QUARTERS), :],
        )
        xs[pl.ds(first * MODES + n, 1), :] = jnp.sum(early, axis=0, keepdims=True)
        return c

    lax.fori_loop(0, part_rows, within_chip, 0, unroll=8)

    def pairs(g, total):
        pair = lax.dot_general(
            prod[g], grad[g], (((1,), (1,)), ((), ())), preferred_element_type=jnp.float32
        )
        hi, lo = split(pair)
        turned = dot(hi, flip) + dot(lo, flip)
        lagged = pltpu.roll(turned, 0, 1, stride=1, stride_axis=0)
        cross = jnp.sum(jnp.where(col >= row, lagged, 0.0), axis=0, keepdims=True)
        rates = group_rates(g)
        chip_part = xs[pl.ds(pl.multiple_of(g * MODES, MODES), MODES), :]
        inside = jnp.exp(-rates * (span - 1.0 - lane)) * cross + jnp.exp(-rates) * chip_part
        inside = jnp.sum(inside, axis=1, keepdims=True)
        return total + jnp.sum(jnp.where(here == g * MODES, inside, 0.0), axis=0, keepdims=True)

    share = lax.fori_loop(0, groups, pairs, jnp.zeros((1, LANES), jnp.float32))

    def reduce_start(level, buf, radix, stride, value):
        digit = lax.rem(lax.div(chip, stride), radix)
        base = chip - digit * stride
        vbuf[level] = value
        buf[digit] = value
        for d in range(1, radix):
            pltpu.make_async_remote_copy(
                src_ref=vbuf.at[level],
                dst_ref=buf.at[digit],
                send_sem=sems.at[4 + 2 * level],
                recv_sem=sems.at[5 + 2 * level],
                device_id=place((base + lax.rem(digit + d, radix) * stride) * 2 + core),
                device_id_type=MESH,
            ).start()

    def reduce_end(level, buf, radix):
        part = buf.at[pl.ds(0, radix - 1)]
        await_all(part, sems.at[5 + 2 * level])
        await_all(part, sems.at[4 + 2 * level])
        return jnp.sum(buf[...], axis=0)

    radix_one = 2 * RING
    radix_two = chips // radix_one
    reduce_start(0, v_one, radix_one, 1, share)

    turned_lags = jnp.where(lane_i == 0, 0, LANES - lane_i).astype(jnp.float32)
    triple = 3 * MODES
    token = iota((span, triple), 0).astype(jnp.float32)
    which = iota((span, triple), 1)

    def local(g, c):
        rates = group_rates(g)
        decay_row = small[0, pl.ds(g, 1), :]
        res_row = small[1, pl.ds(g, 1), :]
        weights = column(res_row)

        def toeplitz(lags, keep):
            line = jnp.sum(weights * jnp.exp(-rates * lags), axis=0, keepdims=True)
            full = pltpu.roll(jnp.broadcast_to(line, (span, LANES)), 0, 1, stride=1, stride_axis=0)
            return jnp.concatenate(split(jnp.where(keep, full, 0.0)), axis=1)

        p = prod[g]
        r = grad[g]
        mixed_ref[g] = dot(toeplitz(turned_lags, row >= col), jnp.concatenate([p, p], axis=0))
        conv_ref[g] = dot(toeplitz(lane, row <= col), jnp.concatenate([r, r], axis=0))
        decay_rows = jnp.concatenate([decay_row] * 3, axis=1)
        res_rows = jnp.concatenate([res_row] * 3, axis=1)

        def table(distance):
            hi, lo = split(res_rows * jnp.exp(-decay_rows * distance))
            return jnp.where(which < 2 * MODES, hi.astype(jnp.float32), lo.astype(jnp.float32)).astype(
                jnp.bfloat16
            )

        rise_ref[g] = table(token + 1.0)
        fall_ref[g] = table(span - token)
        return c

    lax.fori_loop(0, part_groups, local, 0)

    own = tile_at(chip)
    await_all(recv.at[most, :], sems.at[1])
    recv[own, :] = comb[own, :]

    rate = jnp.broadcast_to(acol[pl.ds(first * MODES + chip, 1), :], (QUARTERS, LANES))
    leap = jnp.exp(-rate * (2.0 * span))
    zero = jnp.zeros((QUARTERS, LANES), jnp.float32)

    def step(i, carry):
        rising, falling, acc = carry
        up = pl.multiple_of(i * TILE, TILE)
        down = pl.multiple_of((chips - 1 - i) * TILE, TILE)
        back[i, pl.ds(0, QUARTERS), :] = rising
        back[chips - 1 - i, pl.ds(QUARTERS, QUARTERS), :] = falling
        acc = acc + rising * recv[pl.ds(up + QUARTERS, QUARTERS), :]
        rising = leap * rising + recv[pl.ds(up, QUARTERS), :]
        falling = leap * falling + recv[pl.ds(down + QUARTERS, QUARTERS), :]
        return rising, falling, acc

    rising, falling, acc = lax.fori_loop(0, chips, step, (zero, zero, zero), unroll=8)
    pooled = jnp.sum(jnp.exp(-rate) * acc, axis=0, keepdims=True)
    for t in range(chips):
        back[t, TILE : TILE + 1, :] = pooled
    scatter(lambda t: back.at[t], lambda t: half.at[t], sems.at[2], sems.at[3])
    half[chip] = back[chip]

    share = reduce_end(0, v_one, radix_one)
    reduce_start(1, v_two, radix_two, radix_one, share)
    lax.fori_loop(part_groups, groups, local, 0)

    await_all(half.at[rest], sems.at[3])

    def back_copy(n):
        return pltpu.make_async_remote_copy(
            src_ref=sib.at[pl.ds(n * block, block), :],
            dst_ref=state_ref.at[pl.ds(pl.multiple_of((first + n) * block, block), block), :],
            send_sem=swap_sem.at[1, 0, n],
            recv_sem=swap_sem.at[1, 1, n],
            device_id=place(sibling),
            device_id_type=MESH,
        )

    def for_sibling(n, c):
        x = half[n, pl.ds(0, TILE), :]
        factor = row_factor(n, TILE)
        sib[tile_at(n), :] = jnp.where(lead, factor * x + send[own_tile(n), :], x)
        return c

    def for_me(n, c):
        x = half[n, pl.ds(0, TILE), :]
        factor = row_factor(n, TILE)
        state_ref[own_tile(n), :] = jnp.where(lead, x, factor * x + theirs[tile_at(n), :])
        return c

    for n in range(part_groups):
        lax.fori_loop(n * MODES, (n + 1) * MODES, for_sibling, 0, unroll=8)
        back_copy(n).start()
    share = reduce_end(1, v_two, radix_two)
    pools = jnp.concatenate([half[t, TILE : TILE + 1, :] for t in range(chips)], axis=0)
    pools = jnp.sum(pools, axis=1, keepdims=True)
    spot = iota((chips, LANES), 1) - iota((chips, LANES), 0) == first * MODES
    share = share + jnp.sum(jnp.where(spot, pools, 0.0), axis=0, keepdims=True)
    vbuf[2] = share
    last = pltpu.make_async_remote_copy(
        src_ref=vbuf.at[2],
        dst_ref=v_got.at[0],
        send_sem=sems.at[8],
        recv_sem=sems.at[9],
        device_id=place(sibling),
        device_id_type=MESH,
    )
    last.start()
    lax.fori_loop(0, part_rows, for_me, 0, unroll=8)
    last.wait()
    total_ref[...] = share + v_got[0]

    for n in range(part_groups):
        out_copy(n).wait_send()
        back_copy(n).wait()
    await_all(comb.at[most, :], sems.at[0])
    await_all(back.at[rest], sems.at[2])


def exchange(query_input, key_input, value_input, out_grad, residues, decays):
    inner = lax.axis_size("grp")
    count = lax.axis_size("ctx") * inner
    span, width = query_input.shape
    groups = width // GROUP
    rows = groups * MODES * TILE
    chips = count // 2
    f32 = jnp.float32
    bf16 = jnp.bfloat16

    def body(*refs):
        exchange_kernel(count, groups, span, inner, *refs)

    hbm = pl.BlockSpec(memory_space=pltpu.HBM)
    vmem = pl.BlockSpec(memory_space=pltpu.VMEM)
    return pl.pallas_call(
        body,
        out_shape=(
            jax.ShapeDtypeStruct((rows, LANES), f32),
            jax.ShapeDtypeStruct((1, LANES), f32),
            jax.ShapeDtypeStruct((4, groups, span, GROUP), bf16),
            jax.ShapeDtypeStruct((groups, span, GROUP), f32),
            jax.ShapeDtypeStruct((groups, span, GROUP), f32),
            jax.ShapeDtypeStruct((groups, span, 3 * MODES), bf16),
            jax.ShapeDtypeStruct((groups, span, 3 * MODES), bf16),
        ),
        in_specs=[hbm] * 6,
        out_specs=(vmem,) * 7,
        scratch_shapes=[
            pltpu.VMEM((groups, span, GROUP), bf16),
            pltpu.VMEM((groups, span, GROUP), bf16),
            pltpu.VMEM((rows, LANES), f32),
            pltpu.VMEM((rows // 2, LANES), f32),
            pltpu.VMEM((rows // 2, LANES), f32),
            pltpu.VMEM((chips * TILE, LANES), f32),
            pltpu.VMEM((chips, EXTRA, LANES), f32),
            pltpu.VMEM((chips, EXTRA, LANES), f32),
            pltpu.VMEM((rows // 2, LANES), f32),
            pltpu.VMEM((groups * MODES, LANES), f32),
            pltpu.VMEM((groups * MODES, LANES), f32),
            pltpu.VMEM((2, groups, MODES), f32),
            pltpu.VMEM((3, 1, LANES), f32),
            pltpu.VMEM((2 * RING, 1, LANES), f32),
            pltpu.VMEM((chips // (2 * RING), 1, LANES), f32),
            pltpu.VMEM((1, 1, LANES), f32),
            pltpu.SemaphoreType.DMA((groups, 4)),
            pltpu.SemaphoreType.DMA((2,)),
            pltpu.SemaphoreType.DMA((2, 2, groups // 2)),
            pltpu.SemaphoreType.DMA((10,)),
        ],
        compiler_params=pltpu.CompilerParams(
            collective_id=0, has_side_effects=True, vmem_limit_bytes=20 * MIB
        ),
    )(
        *(
            pltpu.with_memory_space_constraint(a, pltpu.HBM)
            for a in (query_input, key_input, value_input, out_grad, residues, decays)
        )
    )


def finish_kernel(
    groups, scale,
    state_ref, total_ref, ins, mixed_ref, conv_ref, rise_ref, fall_ref,
    out_hbm, qg_hbm, kg_hbm, vg_hbm, rg_ref,
    outs, sems,
):
    targets = (out_hbm, qg_hbm, kg_hbm, vg_hbm)

    def store(g, n):
        return pltpu.make_async_copy(
            outs.at[n, g],
            targets[n].at[:, pl.ds(pl.multiple_of(g * GROUP, GROUP), GROUP)],
            sems.at[n, g],
        )

    def carried(table, g, offset):
        state = jnp.concatenate(
            [
                state_ref[pl.ds(g * MODES * TILE + offset + n, MODES, stride=TILE), :]
                for n in range(QUARTERS)
            ],
            axis=1,
        )
        hi, lo = split(state)
        return dot(table, jnp.concatenate([hi, lo, hi], axis=0))

    def one(g, c):
        mixed = mixed_ref[g] + carried(rise_ref[g], g, 0)
        outs[0, g] = ins[0, g].astype(jnp.float32) * mixed
        store(g, 0).start()
        outs[1, g] = ins[3, g].astype(jnp.float32) * mixed
        store(g, 1).start()
        conv = conv_ref[g] + carried(fall_ref[g], g, QUARTERS)
        outs[2, g] = ins[2, g].astype(jnp.float32) * conv
        store(g, 2).start()
        outs[3, g] = ins[1, g].astype(jnp.float32) * conv
        store(g, 3).start()
        return c

    lax.fori_loop(0, groups, one, 0)

    spread = jnp.broadcast_to(total_ref[...], (groups, LANES))
    own = lax.div(iota((groups, LANES), 1), MODES) == iota((groups, LANES), 0)
    spread = jnp.where(own, spread, 0.0)
    out = spread
    for n in range(1, groups):
        out = out + pltpu.roll(spread, LANES - n * MODES, 1)
    rg_ref[...] = out[:, :MODES] * scale

    for g in range(groups):
        for n in range(4):
            store(g, n).wait()


def finish(parts, span, width, length):
    groups = width // GROUP
    scale = 1.0 / (length * math.sqrt(GROUP))

    def body(*refs):
        finish_kernel(groups, scale, *refs)

    hbm = pl.BlockSpec(memory_space=pltpu.HBM)
    vmem = pl.BlockSpec(memory_space=pltpu.VMEM)
    big = jax.ShapeDtypeStruct((span, width), jnp.float32)
    return pl.pallas_call(
        body,
        out_shape=(big, big, big, big, jax.ShapeDtypeStruct((groups, MODES), jnp.float32)),
        in_specs=[vmem] * 7,
        out_specs=(hbm, hbm, hbm, hbm, vmem),
        scratch_shapes=[
            pltpu.VMEM((4, groups, span, GROUP), jnp.float32),
            pltpu.SemaphoreType.DMA((4, groups)),
        ],
        compiler_params=pltpu.CompilerParams(vmem_limit_bytes=20 * MIB),
    )(*parts)


def on_device(query_input, key_input, value_input, out_grad, residues, decay_rates):
    span, width = query_input.shape
    length = span * lax.axis_size("ctx") * lax.axis_size("grp")
    parts = exchange(query_input, key_input, value_input, out_grad, residues, decay_rates)
    return finish(parts, span, width, length)


def solution(mesh):
    rows = P(("ctx", "grp"), None)
    return jax.shard_map(
        on_device,
        mesh=mesh,
        in_specs=(rows, rows, rows, rows, P(), P()),
        out_specs=(rows, rows, rows, rows, P()),
        check_vma=False,
    )
```

```python
import math

import jax
import jax.numpy as jnp
from jax import lax
from jax.experimental import pallas as pl
from jax.experimental.pallas import tpu as pltpu
from jax.sharding import PartitionSpec as P

GROUP = 512
MODES = 16
LANES = 128
TILE = 8
QUARTERS = GROUP // LANES
RING = 4
EXTRA = TILE + 1
MESH = pl.DeviceIdType.MESH
MIB = 1024 * 1024


def iota(shape, axis):
    return lax.broadcasted_iota(jnp.int32, shape, axis)


def split(x):
    hi = x.astype(jnp.bfloat16)
    lo = (x - hi.astype(jnp.float32)).astype(jnp.bfloat16)
    return hi, lo


def dot(a, b):
    return jnp.dot(a, b, preferred_element_type=jnp.float32)


def column(row):
    eye = iota((MODES, MODES), 0) == iota((MODES, MODES), 1)
    return jnp.sum(jnp.where(eye, jnp.broadcast_to(row, (MODES, MODES)), 0.0), axis=1, keepdims=True)


def gated(a, b):
    return (a.astype(jnp.float32) * b.astype(jnp.float32)).astype(jnp.bfloat16)


FAR_PLANES = (2, 1, 3, 0)
NEAR_PLANES = (0, 1, 3, 2)


def shifts():
    hops = (0, 1, 2, 1)
    every = [(z, y, x) for z in range(RING) for y in range(RING) for x in range(RING)]
    return sorted(every[1:], key=lambda d: -sum(hops[c] for c in d))


def exchange_kernel(
    count, groups, span, inner,
    q_hbm, k_hbm, v_hbm, o_hbm, res_hbm, decay_hbm,
    state_ref, total_ref, ins, mixed_ref, conv_ref, rise_ref, fall_ref,
    prod, grad, send, theirs, comb, recv, back, half, sib, acol, xs, small,
    vbuf, v_one, v_two, v_got,
    load_sem, small_sem, swap_sem, plane_sem, sems,
):
    me = lax.axis_index("ctx") * inner + lax.axis_index("grp")
    chips = count // 2
    chip = lax.div(me, 2)
    core = lax.rem(me, 2)
    sibling = me + 1 - 2 * core
    part_groups = groups // 2
    part_rows = part_groups * MODES
    first = core * part_groups
    other = part_groups - first

    def place(j):
        return (lax.div(j, inner), lax.rem(j, inner))

    sources = (q_hbm, k_hbm, v_hbm, o_hbm)

    def load(g, n):
        return pltpu.make_async_copy(
            sources[n].at[:, pl.ds(pl.multiple_of(g * GROUP, GROUP), GROUP)],
            ins.at[n, g],
            load_sem.at[g, n],
        )

    def ordered(s):
        return jnp.where(s < part_groups, other + s, first + s - part_groups)


    barrier = pltpu.get_barrier_semaphore()
    pl.semaphore_signal(barrier, inc=1, device_id=place(sibling), device_id_type=MESH)

    y_hi = lax.rem(chip, 2)
    x = lax.rem(lax.div(chip, 2), RING)
    y = y_hi * 2 + lax.rem(lax.div(chip, 2 * RING), 2)
    z = lax.div(chip, 4 * RING)

    def peer(d):
        dz, dy, dx = d
        to_z, to_y, to_x = lax.rem(z + dz, RING), lax.rem(y + dy, RING), lax.rem(x + dx, RING)
        return ((to_z * 2 + lax.rem(to_y, 2)) * RING + to_x) * 2 + lax.div(to_y, 2)

    peers = [(d, peer(d)) for d in shifts()]
    for _, t in peers:
        pl.semaphore_signal(
            barrier, inc=1, device_id=place(t * 2 + core), device_id_type=MESH
        )

    tables = [
        pltpu.make_async_copy(decay_hbm, small.at[0], small_sem.at[0]),
        pltpu.make_async_copy(res_hbm, small.at[1], small_sem.at[1]),
    ]
    for copy in tables:
        copy.start()

    for s in range(groups):
        for n in range(4):
            load(ordered(s), n).start()

    lane_i = iota((MODES, LANES), 1)
    lane = lane_i.astype(jnp.float32)
    for copy in tables:
        copy.wait()
    for g in range(groups):
        rates = jnp.broadcast_to(column(small[0, g : g + 1, :]), (MODES, LANES))
        acol[g * MODES : (g + 1) * MODES, :] = rates

    def group_rates(g):
        return acol[pl.ds(pl.multiple_of(g * MODES, MODES), MODES), :]

    block = MODES * TILE

    def swap_copy(source, target, n, where, phase):
        return pltpu.make_async_remote_copy(
            src_ref=source.at[pl.ds(pl.multiple_of(where, block), block), :],
            dst_ref=target.at[pl.ds(pl.multiple_of(n * block, block), block), :],
            send_sem=swap_sem.at[phase, 0, n],
            recv_sem=swap_sem.at[phase, 1, n],
            device_id=place(sibling),
            device_id_type=MESH,
        )

    def plane(d):
        return lax.rem(z + d, RING)

    def out_copy(n):
        return swap_copy(send, theirs, n, (other + n) * block, 0)

    def states(s, c):
        g = ordered(s)
        for n in range(4):
            load(g, n).wait()
        p = gated(ins[1, g], ins[2, g])
        r = gated(ins[3, g], ins[0, g])
        prod[g] = p
        grad[g] = r
        rates = group_rates(g)
        to_end = jnp.concatenate(split(jnp.exp(-rates * (span - 1.0 - lane))), axis=0)
        from_start = jnp.concatenate(split(jnp.exp(-rates * lane)), axis=0)
        ends = dot(to_end, p)
        starts = dot(from_start, r)
        ends = ends[:MODES] + ends[MODES:]
        starts = starts[:MODES] + starts[MODES:]
        for k in range(QUARTERS):
            cut = slice(k * LANES, (k + 1) * LANES)
            send[pl.ds(g * block + k, MODES, stride=TILE), :] = ends[:, cut]
            send[pl.ds(g * block + QUARTERS + k, MODES, stride=TILE), :] = starts[:, cut]
        return c

    lax.fori_loop(0, groups, states, 0)
    pl.semaphore_wait(barrier, chips)
    for d in FAR_PLANES:
        out_copy(plane(d)).start()

    sub = iota((TILE, LANES), 0)
    lead = (sub < QUARTERS) == (core == 0)

    def row_factor(n, width):
        rate = acol[pl.ds(first * MODES + n, 1), :]
        return jnp.broadcast_to(jnp.exp(-rate * float(span)), (width, LANES))

    def sweep(n, one):
        for m in range(MODES):
            one(n * MODES + m, 0)

    def tile_at(n):
        return pl.ds(pl.multiple_of(n * TILE, TILE), TILE)

    def own_tile(n):
        return pl.ds(pl.multiple_of(first * block + n * TILE, TILE), TILE)

    def combine(n, c):
        factor = row_factor(n, TILE)
        mine = send[own_tile(n), :]
        got = theirs[tile_at(n), :]
        comb[tile_at(n), :] = jnp.where(lead, factor, 1.0) * mine + jnp.where(lead, 1.0, factor) * got
        return c

    def message(source, target, t, send_sem, recv_sem):
        return pltpu.make_async_remote_copy(
            src_ref=source,
            dst_ref=target,
            send_sem=send_sem,
            recv_sem=recv_sem,
            device_id=place(t * 2 + core),
            device_id_type=MESH,
        )

    def await_all(part, sem):
        pltpu.make_async_copy(part, part, sem).wait()

    most = pl.ds(0, (chips - 1) * TILE)
    rest = pl.ds(0, chips - 1)
    for d in FAR_PLANES:
        n = plane(d)
        out_copy(n).wait_recv()
        sweep(n, combine)
        for shift, t in peers:
            if shift[0] == d:
                message(
                    comb.at[tile_at(t), :], recv.at[tile_at(chip), :], t, sems.at[0], sems.at[1]
                ).start()

    row = iota((span, LANES), 0)
    col = iota((span, LANES), 1)
    flip = (row + col == span - 1).astype(jnp.bfloat16)
    here = lane_i - iota((MODES, LANES), 0)

    xs[...] = jnp.zeros_like(xs)

    def within_chip(n, c):
        base = pl.multiple_of(first * block + n * TILE, TILE)
        near = pl.multiple_of(n * TILE, TILE)
        early = jnp.where(
            core == 0,
            send[pl.ds(base, QUARTERS), :] * theirs[pl.ds(near + QUARTERS, QUARTERS), :],
            theirs[pl.ds(near, QUARTERS), :] * send[pl.ds(base + QUARTERS, QUARTERS), :],
        )
        xs[pl.ds(first * MODES + n, 1), :] = jnp.sum(early, axis=0, keepdims=True)
        return c

    lax.fori_loop(0, part_rows, within_chip, 0, unroll=8)

    def pairs(g, total):
        pair = lax.dot_general(
            prod[g], grad[g], (((1,), (1,)), ((), ())), preferred_element_type=jnp.float32
        )
        hi, lo = split(pair)
        turned = dot(hi, flip) + dot(lo, flip)
        lagged = pltpu.roll(turned, 0, 1, stride=1, stride_axis=0)
        cross = jnp.sum(jnp.where(col >= row, lagged, 0.0), axis=0, keepdims=True)
        rates = group_rates(g)
        chip_part = xs[pl.ds(pl.multiple_of(g * MODES, MODES), MODES), :]
        inside = jnp.exp(-rates * (span - 1.0 - lane)) * cross + jnp.exp(-rates) * chip_part
        inside = jnp.sum(inside, axis=1, keepdims=True)
        return total + jnp.sum(jnp.where(here == g * MODES, inside, 0.0), axis=0, keepdims=True)

    share = lax.fori_loop(0, groups, pairs, jnp.zeros((1, LANES), jnp.float32))

    def reduce_start(level, buf, radix, stride, value):
        digit = lax.rem(lax.div(chip, stride), radix)
        base = chip - digit * stride
        vbuf[level] = value
        buf[digit] = value
        for d in range(1, radix):
            pltpu.make_async_remote_copy(
                src_ref=vbuf.at[level],
                dst_ref=buf.at[digit],
                send_sem=sems.at[4 + 2 * level],
                recv_sem=sems.at[5 + 2 * level],
                device_id=place((base + lax.rem(digit + d, radix) * stride) * 2 + core),
                device_id_type=MESH,
            ).start()

    def reduce_end(level, buf, radix):
        part = buf.at[pl.ds(0, radix - 1)]
        await_all(part, sems.at[5 + 2 * level])
        await_all(part, sems.at[4 + 2 * level])
        return jnp.sum(buf[...], axis=0)

    radix_one = 2 * RING
    radix_two = chips // radix_one
    reduce_start(0, v_one, radix_one, 1, share)

    turned_lags = jnp.where(lane_i == 0, 0, LANES - lane_i).astype(jnp.float32)
    triple = 3 * MODES
    token = iota((span, triple), 0).astype(jnp.float32)
    which = iota((span, triple), 1)

    def local(g, c):
        rates = group_rates(g)
        decay_row = small[0, pl.ds(g, 1), :]
        res_row = small[1, pl.ds(g, 1), :]
        weights = column(res_row)

        def toeplitz(lags, keep):
            line = jnp.sum(weights * jnp.exp(-rates * lags), axis=0, keepdims=True)
            full = pltpu.roll(jnp.broadcast_to(line, (span, LANES)), 0, 1, stride=1, stride_axis=0)
            return jnp.concatenate(split(jnp.where(keep, full, 0.0)), axis=1)

        p = prod[g]
        r = grad[g]
        mixed_ref[g] = dot(toeplitz(turned_lags, row >= col), jnp.concatenate([p, p], axis=0))
        conv_ref[g] = dot(toeplitz(lane, row <= col), jnp.concatenate([r, r], axis=0))
        decay_rows = jnp.concatenate([decay_row] * 3, axis=1)
        res_rows = jnp.concatenate([res_row] * 3, axis=1)

        def table(distance):
            hi, lo = split(res_rows * jnp.exp(-decay_rows * distance))
            return jnp.where(which < 2 * MODES, hi.astype(jnp.float32), lo.astype(jnp.float32)).astype(
                jnp.bfloat16
            )

        rise_ref[g] = table(token + 1.0)
        fall_ref[g] = table(span - token)
        return c

    lax.fori_loop(0, part_groups, local, 0)

    own = tile_at(chip)
    await_all(recv.at[most, :], sems.at[1])
    recv[own, :] = comb[own, :]

    rate = jnp.broadcast_to(acol[pl.ds(first * MODES + chip, 1), :], (QUARTERS, LANES))
    leap = jnp.exp(-rate * (2.0 * span))
    zero = jnp.zeros((QUARTERS, LANES), jnp.float32)

    def step(i, carry):
        rising, falling, acc = carry
        up = pl.multiple_of(i * TILE, TILE)
        down = pl.multiple_of((chips - 1 - i) * TILE, TILE)
        back[i, pl.ds(0, QUARTERS), :] = rising
        back[chips - 1 - i, pl.ds(QUARTERS, QUARTERS), :] = falling
        acc = acc + rising * recv[pl.ds(up + QUARTERS, QUARTERS), :]
        rising = leap * rising + recv[pl.ds(up, QUARTERS), :]
        falling = leap * falling + recv[pl.ds(down + QUARTERS, QUARTERS), :]
        return rising, falling, acc

    rising, falling, acc = lax.fori_loop(0, chips, step, (zero, zero, zero), unroll=8)
    pooled = jnp.sum(jnp.exp(-rate) * acc, axis=0, keepdims=True)
    for t in range(chips):
        back[t, TILE : TILE + 1, :] = pooled
    for _, t in peers:
        message(back.at[t], half.at[chip], t, sems.at[2], plane_sem.at[z]).start()
    half[chip] = back[chip]

    share = reduce_end(0, v_one, radix_one)
    reduce_start(1, v_two, radix_two, radix_one, share)
    lax.fori_loop(part_groups, groups, local, 0)

    def back_copy(n):
        return pltpu.make_async_remote_copy(
            src_ref=sib.at[pl.ds(pl.multiple_of(n * block, block), block), :],
            dst_ref=state_ref.at[pl.ds(pl.multiple_of((first + n) * block, block), block), :],
            send_sem=swap_sem.at[1, 0, n],
            recv_sem=swap_sem.at[1, 1, n],
            device_id=place(sibling),
            device_id_type=MESH,
        )

    def for_sibling(n, c):
        x = half[n, pl.ds(0, TILE), :]
        factor = row_factor(n, TILE)
        sib[tile_at(n), :] = jnp.where(lead, factor * x + send[own_tile(n), :], x)
        return c

    def for_me(n, c):
        x = half[n, pl.ds(0, TILE), :]
        factor = row_factor(n, TILE)
        state_ref[own_tile(n), :] = jnp.where(lead, x, factor * x + theirs[tile_at(n), :])
        return c

    sum_rows = here - first * MODES
    pooled_share = jnp.zeros((1, LANES), jnp.float32)
    for d in NEAR_PLANES:
        n = plane(d)
        count_in = MODES - 1 if d == 0 else MODES
        await_all(half.at[pl.ds(0, count_in)], plane_sem.at[n])
        sweep(n, for_sibling)
        back_copy(n).start()
        pools = jnp.concatenate(
            [half[n * MODES + m, TILE : TILE + 1, :] for m in range(MODES)], axis=0
        )
        pools = jnp.sum(pools, axis=1, keepdims=True)
        pooled_share = pooled_share + jnp.sum(
            jnp.where(sum_rows == n * MODES, pools, 0.0), axis=0, keepdims=True
        )
        if d != NEAR_PLANES[-1]:
            sweep(n, for_me)

    share = reduce_end(1, v_two, radix_two) + pooled_share
    vbuf[2] = share
    last = pltpu.make_async_remote_copy(
        src_ref=vbuf.at[2],
        dst_ref=v_got.at[0],
        send_sem=sems.at[8],
        recv_sem=sems.at[9],
        device_id=place(sibling),
        device_id_type=MESH,
    )
    last.start()
    n = plane(NEAR_PLANES[-1])
    sweep(n, for_me)
    last.wait()
    total_ref[...] = share + v_got[0]

    for n in range(part_groups):
        out_copy(n).wait_send()
        back_copy(n).wait()
    await_all(comb.at[most, :], sems.at[0])
    await_all(back.at[rest], sems.at[2])


def exchange(query_input, key_input, value_input, out_grad, residues, decays):
    inner = lax.axis_size("grp")
    count = lax.axis_size("ctx") * inner
    span, width = query_input.shape
    groups = width // GROUP
    rows = groups * MODES * TILE
    chips = count // 2
    f32 = jnp.float32
    bf16 = jnp.bfloat16

    def body(*refs):
        exchange_kernel(count, groups, span, inner, *refs)

    hbm = pl.BlockSpec(memory_space=pltpu.HBM)
    vmem = pl.BlockSpec(memory_space=pltpu.VMEM)
    return pl.pallas_call(
        body,
        out_shape=(
            jax.ShapeDtypeStruct((rows, LANES), f32),
            jax.ShapeDtypeStruct((1, LANES), f32),
            jax.ShapeDtypeStruct((4, groups, span, GROUP), bf16),
            jax.ShapeDtypeStruct((groups, span, GROUP), f32),
            jax.ShapeDtypeStruct((groups, span, GROUP), f32),
            jax.ShapeDtypeStruct((groups, span, 3 * MODES), bf16),
            jax.ShapeDtypeStruct((groups, span, 3 * MODES), bf16),
        ),
        in_specs=[hbm] * 6,
        out_specs=(vmem,) * 7,
        scratch_shapes=[
            pltpu.VMEM((groups, span, GROUP), bf16),
            pltpu.VMEM((groups, span, GROUP), bf16),
            pltpu.VMEM((rows, LANES), f32),
            pltpu.VMEM((rows // 2, LANES), f32),
            pltpu.VMEM((rows // 2, LANES), f32),
            pltpu.VMEM((chips * TILE, LANES), f32),
            pltpu.VMEM((chips, EXTRA, LANES), f32),
            pltpu.VMEM((chips, EXTRA, LANES), f32),
            pltpu.VMEM((rows // 2, LANES), f32),
            pltpu.VMEM((groups * MODES, LANES), f32),
            pltpu.VMEM((groups * MODES, LANES), f32),
            pltpu.VMEM((2, groups, MODES), f32),
            pltpu.VMEM((3, 1, LANES), f32),
            pltpu.VMEM((2 * RING, 1, LANES), f32),
            pltpu.VMEM((chips // (2 * RING), 1, LANES), f32),
            pltpu.VMEM((1, 1, LANES), f32),
            pltpu.SemaphoreType.DMA((groups, 4)),
            pltpu.SemaphoreType.DMA((2,)),
            pltpu.SemaphoreType.DMA((2, 2, groups // 2)),
            pltpu.SemaphoreType.DMA((RING,)),
            pltpu.SemaphoreType.DMA((10,)),
        ],
        compiler_params=pltpu.CompilerParams(
            collective_id=0, has_side_effects=True, vmem_limit_bytes=20 * MIB
        ),
    )(
        *(
            pltpu.with_memory_space_constraint(a, pltpu.HBM)
            for a in (query_input, key_input, value_input, out_grad, residues, decays)
        )
    )


def finish_kernel(
    groups, scale,
    state_ref, total_ref, ins, mixed_ref, conv_ref, rise_ref, fall_ref,
    out_hbm, qg_hbm, kg_hbm, vg_hbm, rg_hbm,
    outs, rg_ref, sems, rg_sem,
):
    targets = (out_hbm, qg_hbm, kg_hbm, vg_hbm)

    def store(g, n):
        return pltpu.make_async_copy(
            outs.at[n, g],
            targets[n].at[:, pl.ds(pl.multiple_of(g * GROUP, GROUP), GROUP)],
            sems.at[n, g],
        )

    def carried(table, g, offset):
        state = jnp.concatenate(
            [
                state_ref[pl.ds(g * MODES * TILE + offset + n, MODES, stride=TILE), :]
                for n in range(QUARTERS)
            ],
            axis=1,
        )
        hi, lo = split(state)
        return dot(table, jnp.concatenate([hi, lo, hi], axis=0))

    def one(g, c):
        mixed = mixed_ref[g] + carried(rise_ref[g], g, 0)
        outs[0, g] = ins[0, g].astype(jnp.float32) * mixed
        store(g, 0).start()
        outs[1, g] = ins[3, g].astype(jnp.float32) * mixed
        store(g, 1).start()
        conv = conv_ref[g] + carried(fall_ref[g], g, QUARTERS)
        outs[2, g] = ins[2, g].astype(jnp.float32) * conv
        store(g, 2).start()
        outs[3, g] = ins[1, g].astype(jnp.float32) * conv
        store(g, 3).start()
        return c

    lax.fori_loop(0, groups, one, 0)

    spread = jnp.broadcast_to(total_ref[...], (groups, LANES))
    own = lax.div(iota((groups, LANES), 1), MODES) == iota((groups, LANES), 0)
    spread = jnp.where(own, spread, 0.0)
    out = spread
    for n in range(1, groups):
        out = out + pltpu.roll(spread, LANES - n * MODES, 1)
    rg_ref[...] = out[:, :MODES] * scale
    small = pltpu.make_async_copy(rg_ref, rg_hbm, rg_sem)
    small.start()

    for g in range(groups):
        for n in range(4):
            store(g, n).wait()
    small.wait()


def finish(parts, span, width, length):
    groups = width // GROUP
    scale = 1.0 / (length * math.sqrt(GROUP))

    def body(*refs):
        finish_kernel(groups, scale, *refs)

    hbm = pl.BlockSpec(memory_space=pltpu.HBM)
    vmem = pl.BlockSpec(memory_space=pltpu.VMEM)
    big = jax.ShapeDtypeStruct((span, width), jnp.float32)
    return pl.pallas_call(
        body,
        out_shape=(big, big, big, big, jax.ShapeDtypeStruct((groups, MODES), jnp.float32)),
        in_specs=[vmem] * 7,
        out_specs=(hbm,) * 5,
        scratch_shapes=[
            pltpu.VMEM((4, groups, span, GROUP), jnp.float32),
            pltpu.VMEM((groups, MODES), jnp.float32),
            pltpu.SemaphoreType.DMA((4, groups)),
            pltpu.SemaphoreType.DMA(()),
        ],
        compiler_params=pltpu.CompilerParams(vmem_limit_bytes=20 * MIB),
    )(*parts)


def on_device(query_input, key_input, value_input, out_grad, residues, decay_rates):
    span, width = query_input.shape
    length = span * lax.axis_size("ctx") * lax.axis_size("grp")
    parts = exchange(query_input, key_input, value_input, out_grad, residues, decay_rates)
    return finish(parts, span, width, length)


def solution(mesh):
    rows = P(("ctx", "grp"), None)
    return jax.shard_map(
        on_device,
        mesh=mesh,
        in_specs=(rows, rows, rows, rows, P(), P()),
        out_specs=(rows, rows, rows, rows, P()),
        check_vma=False,
    )
```

```python
import math

import jax
import jax.numpy as jnp
from jax import lax
from jax.experimental import pallas as pl
from jax.experimental.pallas import tpu as pltpu
from jax.sharding import PartitionSpec as P

GROUP = 512
MODES = 16
LANES = 128
TILE = 8
QUARTERS = GROUP // LANES
RING = 4
EXTRA = TILE + 1
MESH = pl.DeviceIdType.MESH
MIB = 1024 * 1024


def iota(shape, axis):
    return lax.broadcasted_iota(jnp.int32, shape, axis)


def split(x):
    hi = x.astype(jnp.bfloat16)
    lo = (x - hi.astype(jnp.float32)).astype(jnp.bfloat16)
    return hi, lo


def dot(a, b):
    return jnp.dot(a, b, preferred_element_type=jnp.float32)


def column(row):
    eye = iota((MODES, MODES), 0) == iota((MODES, MODES), 1)
    return jnp.sum(jnp.where(eye, jnp.broadcast_to(row, (MODES, MODES)), 0.0), axis=1, keepdims=True)


def gated(a, b):
    return (a.astype(jnp.float32) * b.astype(jnp.float32)).astype(jnp.bfloat16)


FAR_PLANES = (2, 1, 3, 0)
NEAR_PLANES = (0, 1, 3, 2)


def shifts():
    hops = (0, 1, 2, 1)
    every = [(z, y, x) for z in range(RING) for y in range(RING) for x in range(RING)]
    return sorted(every[1:], key=lambda d: -sum(hops[c] for c in d))


def exchange_kernel(
    count, groups, span, inner,
    q_hbm, k_hbm, v_hbm, o_hbm, res_hbm, decay_hbm,
    state_ref, total_ref, ins, mixed_ref, conv_ref, rise_ref, fall_ref,
    prod, grad, send, theirs, comb, recv, back, half, sib, acol, xs, small,
    vbuf, v_one, v_two, v_got,
    load_sem, small_sem, swap_sem, plane_sem, sems,
):
    me = lax.axis_index("ctx") * inner + lax.axis_index("grp")
    chips = count // 2
    chip = lax.div(me, 2)
    core = lax.rem(me, 2)
    sibling = me + 1 - 2 * core
    part_groups = groups // 2
    part_rows = part_groups * MODES
    first = core * part_groups
    other = part_groups - first

    def place(j):
        return (lax.div(j, inner), lax.rem(j, inner))

    sources = (q_hbm, k_hbm, v_hbm, o_hbm)

    def load(g, n):
        return pltpu.make_async_copy(
            sources[n].at[:, pl.ds(pl.multiple_of(g * GROUP, GROUP), GROUP)],
            ins.at[n, g],
            load_sem.at[g, n],
        )

    def ordered(s):
        return jnp.where(s < part_groups, other + s, first + s - part_groups)


    barrier = pltpu.get_barrier_semaphore()
    pl.semaphore_signal(barrier, inc=1, device_id=place(sibling), device_id_type=MESH)

    y_hi = lax.rem(chip, 2)
    x = lax.rem(lax.div(chip, 2), RING)
    y = y_hi * 2 + lax.rem(lax.div(chip, 2 * RING), 2)
    z = lax.div(chip, 4 * RING)

    def peer(d):
        dz, dy, dx = d
        to_z, to_y, to_x = lax.rem(z + dz, RING), lax.rem(y + dy, RING), lax.rem(x + dx, RING)
        return ((to_z * 2 + lax.rem(to_y, 2)) * RING + to_x) * 2 + lax.div(to_y, 2)

    peers = [(d, peer(d)) for d in shifts()]
    for _, t in peers:
        pl.semaphore_signal(
            barrier, inc=1, device_id=place(t * 2 + core), device_id_type=MESH
        )

    tables = [
        pltpu.make_async_copy(decay_hbm, small.at[0], small_sem.at[0]),
        pltpu.make_async_copy(res_hbm, small.at[1], small_sem.at[1]),
    ]
    for copy in tables:
        copy.start()

    for s in range(groups):
        for n in range(4):
            load(ordered(s), n).start()

    lane_i = iota((MODES, LANES), 1)
    lane = lane_i.astype(jnp.float32)
    for copy in tables:
        copy.wait()
    for g in range(groups):
        rates = jnp.broadcast_to(column(small[0, g : g + 1, :]), (MODES, LANES))
        acol[g * MODES : (g + 1) * MODES, :] = rates

    def group_rates(g):
        return acol[pl.ds(pl.multiple_of(g * MODES, MODES), MODES), :]

    block = MODES * TILE

    def swap_copy(source, target, n, where, phase):
        return pltpu.make_async_remote_copy(
            src_ref=source.at[pl.ds(pl.multiple_of(where, block), block), :],
            dst_ref=target.at[pl.ds(pl.multiple_of(n * block, block), block), :],
            send_sem=swap_sem.at[phase, 0, n],
            recv_sem=swap_sem.at[phase, 1, n],
            device_id=place(sibling),
            device_id_type=MESH,
        )

    def plane(d):
        return lax.rem(z + d, RING)

    def out_copy(n):
        return swap_copy(send, theirs, n, (other + n) * block, 0)

    def states(s, c):
        g = ordered(s)
        for n in range(4):
            load(g, n).wait()
        p = gated(ins[1, g], ins[2, g])
        r = gated(ins[3, g], ins[0, g])
        prod[g] = p
        grad[g] = r
        rates = group_rates(g)
        to_end = jnp.concatenate(split(jnp.exp(-rates * (span - 1.0 - lane))), axis=0)
        from_start = jnp.concatenate(split(jnp.exp(-rates * lane)), axis=0)
        ends = dot(to_end, p)
        starts = dot(from_start, r)
        ends = ends[:MODES] + ends[MODES:]
        starts = starts[:MODES] + starts[MODES:]
        for k in range(QUARTERS):
            cut = slice(k * LANES, (k + 1) * LANES)
            send[pl.ds(g * block + k, MODES, stride=TILE), :] = ends[:, cut]
            send[pl.ds(g * block + QUARTERS + k, MODES, stride=TILE), :] = starts[:, cut]
        return c

    for s in range(groups):
        states(s, 0)
    pl.semaphore_wait(barrier, chips)
    for d in FAR_PLANES:
        out_copy(plane(d)).start()

    sub = iota((TILE, LANES), 0)
    lead = (sub < QUARTERS) == (core == 0)

    def row_factor(n, width):
        rate = acol[pl.ds(first * MODES + n, 1), :]
        return jnp.broadcast_to(jnp.exp(-rate * float(span)), (width, LANES))

    def sweep(n, one):
        for m in range(MODES):
            one(n * MODES + m, 0)

    def tile_at(n):
        return pl.ds(pl.multiple_of(n * TILE, TILE), TILE)

    def own_tile(n):
        return pl.ds(pl.multiple_of(first * block + n * TILE, TILE), TILE)

    def combine(n, c):
        factor = row_factor(n, TILE)
        mine = send[own_tile(n), :]
        got = theirs[tile_at(n), :]
        comb[tile_at(n), :] = jnp.where(lead, factor, 1.0) * mine + jnp.where(lead, 1.0, factor) * got
        return c

    def message(source, target, t, send_sem, recv_sem):
        return pltpu.make_async_remote_copy(
            src_ref=source,
            dst_ref=target,
            send_sem=send_sem,
            recv_sem=recv_sem,
            device_id=place(t * 2 + core),
            device_id_type=MESH,
        )

    def await_all(part, sem):
        pltpu.make_async_copy(part, part, sem).wait()

    most = pl.ds(0, (chips - 1) * TILE)
    rest = pl.ds(0, chips - 1)
    for d in FAR_PLANES:
        n = plane(d)
        out_copy(n).wait_recv()
        sweep(n, combine)
        for shift, t in peers:
            if shift[0] == d:
                message(
                    comb.at[tile_at(t), :], recv.at[tile_at(chip), :], t, sems.at[0], sems.at[1]
                ).start()

    row = iota((span, LANES), 0)
    col = iota((span, LANES), 1)
    flip = (row + col == span - 1).astype(jnp.bfloat16)
    here = lane_i - iota((MODES, LANES), 0)

    xs[...] = jnp.zeros_like(xs)

    def within_chip(n, c):
        base = pl.multiple_of(first * block + n * TILE, TILE)
        near = pl.multiple_of(n * TILE, TILE)
        early = jnp.where(
            core == 0,
            send[pl.ds(base, QUARTERS), :] * theirs[pl.ds(near + QUARTERS, QUARTERS), :],
            theirs[pl.ds(near, QUARTERS), :] * send[pl.ds(base + QUARTERS, QUARTERS), :],
        )
        xs[pl.ds(first * MODES + n, 1), :] = jnp.sum(early, axis=0, keepdims=True)
        return c

    lax.fori_loop(0, part_rows, within_chip, 0, unroll=8)

    def pairs(g, total):
        pair = lax.dot_general(
            prod[g], grad[g], (((1,), (1,)), ((), ())), preferred_element_type=jnp.float32
        )
        hi, lo = split(pair)
        turned = dot(hi, flip) + dot(lo, flip)
        lagged = pltpu.roll(turned, 0, 1, stride=1, stride_axis=0)
        cross = jnp.sum(jnp.where(col >= row, lagged, 0.0), axis=0, keepdims=True)
        rates = group_rates(g)
        chip_part = xs[pl.ds(pl.multiple_of(g * MODES, MODES), MODES), :]
        inside = jnp.exp(-rates * (span - 1.0 - lane)) * cross + jnp.exp(-rates) * chip_part
        inside = jnp.sum(inside, axis=1, keepdims=True)
        return total + jnp.sum(jnp.where(here == g * MODES, inside, 0.0), axis=0, keepdims=True)

    share = lax.fori_loop(0, groups, pairs, jnp.zeros((1, LANES), jnp.float32), unroll=4)

    def reduce_start(level, buf, radix, stride, value):
        digit = lax.rem(lax.div(chip, stride), radix)
        base = chip - digit * stride
        vbuf[level] = value
        buf[digit] = value
        for d in range(1, radix):
            pltpu.make_async_remote_copy(
                src_ref=vbuf.at[level],
                dst_ref=buf.at[digit],
                send_sem=sems.at[4 + 2 * level],
                recv_sem=sems.at[5 + 2 * level],
                device_id=place((base + lax.rem(digit + d, radix) * stride) * 2 + core),
                device_id_type=MESH,
            ).start()

    def reduce_end(level, buf, radix):
        part = buf.at[pl.ds(0, radix - 1)]
        await_all(part, sems.at[5 + 2 * level])
        await_all(part, sems.at[4 + 2 * level])
        return jnp.sum(buf[...], axis=0)

    radix_one = 2 * RING
    radix_two = chips // radix_one
    reduce_start(0, v_one, radix_one, 1, share)

    turned_lags = jnp.where(lane_i == 0, 0, LANES - lane_i).astype(jnp.float32)
    triple = 3 * MODES
    token = iota((span, triple), 0).astype(jnp.float32)
    which = iota((span, triple), 1)

    def local(g, c):
        rates = group_rates(g)
        decay_row = small[0, pl.ds(g, 1), :]
        res_row = small[1, pl.ds(g, 1), :]
        weights = column(res_row)

        def toeplitz(lags, keep):
            line = jnp.sum(weights * jnp.exp(-rates * lags), axis=0, keepdims=True)
            full = pltpu.roll(jnp.broadcast_to(line, (span, LANES)), 0, 1, stride=1, stride_axis=0)
            return jnp.concatenate(split(jnp.where(keep, full, 0.0)), axis=1)

        p = prod[g]
        r = grad[g]
        mixed_ref[g] = dot(toeplitz(turned_lags, row >= col), jnp.concatenate([p, p], axis=0))
        conv_ref[g] = dot(toeplitz(lane, row <= col), jnp.concatenate([r, r], axis=0))
        decay_rows = jnp.concatenate([decay_row] * 3, axis=1)
        res_rows = jnp.concatenate([res_row] * 3, axis=1)

        def table(distance):
            hi, lo = split(res_rows * jnp.exp(-decay_rows * distance))
            return jnp.where(which < 2 * MODES, hi.astype(jnp.float32), lo.astype(jnp.float32)).astype(
                jnp.bfloat16
            )

        rise_ref[g] = table(token + 1.0)
        fall_ref[g] = table(span - token)
        return c

    lax.fori_loop(0, part_groups, local, 0, unroll=2)

    own = tile_at(chip)
    await_all(recv.at[most, :], sems.at[1])
    recv[own, :] = comb[own, :]

    rate = jnp.broadcast_to(acol[pl.ds(first * MODES + chip, 1), :], (QUARTERS, LANES))
    leap = jnp.exp(-rate * (2.0 * span))
    zero = jnp.zeros((QUARTERS, LANES), jnp.float32)

    def step(i, carry):
        rising, falling, acc = carry
        up = pl.multiple_of(i * TILE, TILE)
        down = pl.multiple_of((chips - 1 - i) * TILE, TILE)
        back[i, pl.ds(0, QUARTERS), :] = rising
        back[chips - 1 - i, pl.ds(QUARTERS, QUARTERS), :] = falling
        acc = acc + rising * recv[pl.ds(up + QUARTERS, QUARTERS), :]
        rising = leap * rising + recv[pl.ds(up, QUARTERS), :]
        falling = leap * falling + recv[pl.ds(down + QUARTERS, QUARTERS), :]
        return rising, falling, acc

    rising, falling, acc = lax.fori_loop(0, chips, step, (zero, zero, zero), unroll=8)
    pooled = jnp.sum(jnp.exp(-rate) * acc, axis=0, keepdims=True)
    for t in range(chips):
        back[t, TILE : TILE + 1, :] = pooled
    for _, t in peers:
        message(back.at[t], half.at[chip], t, sems.at[2], plane_sem.at[z]).start()
    half[chip] = back[chip]

    share = reduce_end(0, v_one, radix_one)
    reduce_start(1, v_two, radix_two, radix_one, share)
    lax.fori_loop(part_groups, groups, local, 0, unroll=2)

    def back_copy(n):
        return pltpu.make_async_remote_copy(
            src_ref=sib.at[pl.ds(pl.multiple_of(n * block, block), block), :],
            dst_ref=state_ref.at[pl.ds(pl.multiple_of((first + n) * block, block), block), :],
            send_sem=swap_sem.at[1, 0, n],
            recv_sem=swap_sem.at[1, 1, n],
            device_id=place(sibling),
            device_id_type=MESH,
        )

    def for_sibling(n, c):
        x = half[n, pl.ds(0, TILE), :]
        factor = row_factor(n, TILE)
        sib[tile_at(n), :] = jnp.where(lead, factor * x + send[own_tile(n), :], x)
        return c

    def for_me(n, c):
        x = half[n, pl.ds(0, TILE), :]
        factor = row_factor(n, TILE)
        state_ref[own_tile(n), :] = jnp.where(lead, x, factor * x + theirs[tile_at(n), :])
        return c

    sum_rows = here - first * MODES
    pooled_share = jnp.zeros((1, LANES), jnp.float32)
    for d in NEAR_PLANES:
        n = plane(d)
        count_in = MODES - 1 if d == 0 else MODES
        await_all(half.at[pl.ds(0, count_in)], plane_sem.at[n])
        sweep(n, for_sibling)
        back_copy(n).start()
        pools = jnp.concatenate(
            [half[n * MODES + m, TILE : TILE + 1, :] for m in range(MODES)], axis=0
        )
        pools = jnp.sum(pools, axis=1, keepdims=True)
        pooled_share = pooled_share + jnp.sum(
            jnp.where(sum_rows == n * MODES, pools, 0.0), axis=0, keepdims=True
        )
        if d != NEAR_PLANES[-1]:
            sweep(n, for_me)

    share = reduce_end(1, v_two, radix_two) + pooled_share
    vbuf[2] = share
    last = pltpu.make_async_remote_copy(
        src_ref=vbuf.at[2],
        dst_ref=v_got.at[0],
        send_sem=sems.at[8],
        recv_sem=sems.at[9],
        device_id=place(sibling),
        device_id_type=MESH,
    )
    last.start()
    n = plane(NEAR_PLANES[-1])
    sweep(n, for_me)
    last.wait()
    total_ref[...] = share + v_got[0]

    for n in range(part_groups):
        out_copy(n).wait_send()
        back_copy(n).wait()
    await_all(comb.at[most, :], sems.at[0])
    await_all(back.at[rest], sems.at[2])


def exchange(query_input, key_input, value_input, out_grad, residues, decays):
    inner = lax.axis_size("grp")
    count = lax.axis_size("ctx") * inner
    span, width = query_input.shape
    groups = width // GROUP
    rows = groups * MODES * TILE
    chips = count // 2
    f32 = jnp.float32
    bf16 = jnp.bfloat16

    def body(*refs):
        exchange_kernel(count, groups, span, inner, *refs)

    hbm = pl.BlockSpec(memory_space=pltpu.HBM)
    vmem = pl.BlockSpec(memory_space=pltpu.VMEM)
    return pl.pallas_call(
        body,
        out_shape=(
            jax.ShapeDtypeStruct((rows, LANES), f32),
            jax.ShapeDtypeStruct((1, LANES), f32),
            jax.ShapeDtypeStruct((4, groups, span, GROUP), bf16),
            jax.ShapeDtypeStruct((groups, span, GROUP), f32),
            jax.ShapeDtypeStruct((groups, span, GROUP), f32),
            jax.ShapeDtypeStruct((groups, span, 3 * MODES), bf16),
            jax.ShapeDtypeStruct((groups, span, 3 * MODES), bf16),
        ),
        in_specs=[hbm] * 6,
        out_specs=(vmem,) * 7,
        scratch_shapes=[
            pltpu.VMEM((groups, span, GROUP), bf16),
            pltpu.VMEM((groups, span, GROUP), bf16),
            pltpu.VMEM((rows, LANES), f32),
            pltpu.VMEM((rows // 2, LANES), f32),
            pltpu.VMEM((rows // 2, LANES), f32),
            pltpu.VMEM((chips * TILE, LANES), f32),
            pltpu.VMEM((chips, EXTRA, LANES), f32),
            pltpu.VMEM((chips, EXTRA, LANES), f32),
            pltpu.VMEM((rows // 2, LANES), f32),
            pltpu.VMEM((groups * MODES, LANES), f32),
            pltpu.VMEM((groups * MODES, LANES), f32),
            pltpu.VMEM((2, groups, MODES), f32),
            pltpu.VMEM((3, 1, LANES), f32),
            pltpu.VMEM((2 * RING, 1, LANES), f32),
            pltpu.VMEM((chips // (2 * RING), 1, LANES), f32),
            pltpu.VMEM((1, 1, LANES), f32),
            pltpu.SemaphoreType.DMA((groups, 4)),
            pltpu.SemaphoreType.DMA((2,)),
            pltpu.SemaphoreType.DMA((2, 2, groups // 2)),
            pltpu.SemaphoreType.DMA((RING,)),
            pltpu.SemaphoreType.DMA((10,)),
        ],
        compiler_params=pltpu.CompilerParams(
            collective_id=0, has_side_effects=True, vmem_limit_bytes=20 * MIB
        ),
    )(
        *(
            pltpu.with_memory_space_constraint(a, pltpu.HBM)
            for a in (query_input, key_input, value_input, out_grad, residues, decays)
        )
    )


def finish_kernel(
    groups, scale,
    state_ref, total_ref, ins, mixed_ref, conv_ref, rise_ref, fall_ref,
    out_hbm, qg_hbm, kg_hbm, vg_hbm, rg_hbm,
    outs, rg_ref, sems, rg_sem,
):
    targets = (out_hbm, qg_hbm, kg_hbm, vg_hbm)

    def store(g, n):
        return pltpu.make_async_copy(
            outs.at[n, g],
            targets[n].at[:, pl.ds(pl.multiple_of(g * GROUP, GROUP), GROUP)],
            sems.at[n, g],
        )

    def carried(table, g, offset):
        state = jnp.concatenate(
            [
                state_ref[pl.ds(g * MODES * TILE + offset + n, MODES, stride=TILE), :]
                for n in range(QUARTERS)
            ],
            axis=1,
        )
        hi, lo = split(state)
        return dot(table, jnp.concatenate([hi, lo, hi], axis=0))

    def one(g, c):
        mixed = mixed_ref[g] + carried(rise_ref[g], g, 0)
        outs[0, g] = ins[0, g].astype(jnp.float32) * mixed
        store(g, 0).start()
        outs[1, g] = ins[3, g].astype(jnp.float32) * mixed
        store(g, 1).start()
        conv = conv_ref[g] + carried(fall_ref[g], g, QUARTERS)
        outs[2, g] = ins[2, g].astype(jnp.float32) * conv
        store(g, 2).start()
        outs[3, g] = ins[1, g].astype(jnp.float32) * conv
        store(g, 3).start()
        return c

    for g in range(groups):
        one(g, 0)

    spread = jnp.broadcast_to(total_ref[...], (groups, LANES))
    own = lax.div(iota((groups, LANES), 1), MODES) == iota((groups, LANES), 0)
    spread = jnp.where(own, spread, 0.0)
    out = spread
    for n in range(1, groups):
        out = out + pltpu.roll(spread, LANES - n * MODES, 1)
    rg_ref[...] = out[:, :MODES] * scale
    small = pltpu.make_async_copy(rg_ref, rg_hbm, rg_sem)
    small.start()

    for g in range(groups):
        for n in range(4):
            store(g, n).wait()
    small.wait()


def finish(parts, span, width, length):
    groups = width // GROUP
    scale = 1.0 / (length * math.sqrt(GROUP))

    def body(*refs):
        finish_kernel(groups, scale, *refs)

    hbm = pl.BlockSpec(memory_space=pltpu.HBM)
    vmem = pl.BlockSpec(memory_space=pltpu.VMEM)
    big = jax.ShapeDtypeStruct((span, width), jnp.float32)
    return pl.pallas_call(
        body,
        out_shape=(big, big, big, big, jax.ShapeDtypeStruct((groups, MODES), jnp.float32)),
        in_specs=[vmem] * 7,
        out_specs=(hbm,) * 5,
        scratch_shapes=[
            pltpu.VMEM((4, groups, span, GROUP), jnp.float32),
            pltpu.VMEM((groups, MODES), jnp.float32),
            pltpu.SemaphoreType.DMA((4, groups)),
            pltpu.SemaphoreType.DMA(()),
        ],
        compiler_params=pltpu.CompilerParams(vmem_limit_bytes=20 * MIB),
    )(*parts)


def on_device(query_input, key_input, value_input, out_grad, residues, decay_rates):
    span, width = query_input.shape
    length = span * lax.axis_size("ctx") * lax.axis_size("grp")
    parts = exchange(query_input, key_input, value_input, out_grad, residues, decay_rates)
    return finish(parts, span, width, length)


def solution(mesh):
    rows = P(("ctx", "grp"), None)
    return jax.shard_map(
        on_device,
        mesh=mesh,
        in_specs=(rows, rows, rows, rows, P(), P()),
        out_specs=(rows, rows, rows, rows, P()),
        check_vma=False,
    )
```

```python
import math

import jax
import jax.numpy as jnp
from jax import lax
from jax.experimental import pallas as pl
from jax.experimental.pallas import tpu as pltpu
from jax.sharding import PartitionSpec as P

GROUP = 512
MODES = 16
LANES = 128
TILE = 8
QUARTERS = GROUP // LANES
RING = 4
EXTRA = TILE + 1
MESH = pl.DeviceIdType.MESH
MIB = 1024 * 1024


def iota(shape, axis):
    return lax.broadcasted_iota(jnp.int32, shape, axis)


def split(x):
    hi = x.astype(jnp.bfloat16)
    lo = (x - hi.astype(jnp.float32)).astype(jnp.bfloat16)
    return hi, lo


def dot(a, b):
    return jnp.dot(a, b, preferred_element_type=jnp.float32)


def column(row):
    eye = iota((MODES, MODES), 0) == iota((MODES, MODES), 1)
    return jnp.sum(jnp.where(eye, jnp.broadcast_to(row, (MODES, MODES)), 0.0), axis=1, keepdims=True)


def gated(a, b):
    return (a.astype(jnp.float32) * b.astype(jnp.float32)).astype(jnp.bfloat16)


FAR_PLANES = (2, 1, 3, 0)
NEAR_PLANES = (0, 1, 3, 2)


def shifts():
    hops = (0, 1, 2, 1)
    every = [(z, y, x) for z in range(RING) for y in range(RING) for x in range(RING)]
    return sorted(every[1:], key=lambda d: -sum(hops[c] for c in d))


def exchange_kernel(
    count, groups, span, inner,
    q_hbm, k_hbm, v_hbm, o_hbm, res_hbm, decay_hbm,
    state_ref, total_ref, ins, mixed_ref, conv_ref, rise_ref, fall_ref,
    prod, grad, send, theirs, comb, recv, back, half, sib, acol, xs, small,
    vbuf, v_one, v_two, v_got,
    load_sem, small_sem, swap_sem, plane_sem, sems,
):
    me = lax.axis_index("ctx") * inner + lax.axis_index("grp")
    chips = count // 2
    chip = lax.div(me, 2)
    core = lax.rem(me, 2)
    sibling = me + 1 - 2 * core
    part_groups = groups // 2
    part_rows = part_groups * MODES
    first = core * part_groups
    other = part_groups - first

    def place(j):
        return (lax.div(j, inner), lax.rem(j, inner))

    sources = (q_hbm, k_hbm, v_hbm, o_hbm)

    def load(g, n):
        return pltpu.make_async_copy(
            sources[n].at[:, pl.ds(pl.multiple_of(g * GROUP, GROUP), GROUP)],
            ins.at[n, g],
            load_sem.at[g, n],
        )

    def ordered(s):
        return jnp.where(s < part_groups, other + s, first + s - part_groups)


    barrier = pltpu.get_barrier_semaphore()
    pl.semaphore_signal(barrier, inc=1, device_id=place(sibling), device_id_type=MESH)

    y_hi = lax.rem(chip, 2)
    x = lax.rem(lax.div(chip, 2), RING)
    y = y_hi * 2 + lax.rem(lax.div(chip, 2 * RING), 2)
    z = lax.div(chip, 4 * RING)

    def peer(d):
        dz, dy, dx = d
        to_z, to_y, to_x = lax.rem(z + dz, RING), lax.rem(y + dy, RING), lax.rem(x + dx, RING)
        return ((to_z * 2 + lax.rem(to_y, 2)) * RING + to_x) * 2 + lax.div(to_y, 2)

    peers = [(d, peer(d)) for d in shifts()]
    for _, t in peers:
        pl.semaphore_signal(
            barrier, inc=1, device_id=place(t * 2 + core), device_id_type=MESH
        )

    tables = [
        pltpu.make_async_copy(decay_hbm, small.at[0], small_sem.at[0]),
        pltpu.make_async_copy(res_hbm, small.at[1], small_sem.at[1]),
    ]
    for copy in tables:
        copy.start()

    for s in range(groups):
        for n in range(4):
            load(ordered(s), n).start()

    lane_i = iota((MODES, LANES), 1)
    lane = lane_i.astype(jnp.float32)
    for copy in tables:
        copy.wait()
    for g in range(groups):
        rates = jnp.broadcast_to(column(small[0, g : g + 1, :]), (MODES, LANES))
        acol[g * MODES : (g + 1) * MODES, :] = rates

    def group_rates(g):
        return acol[pl.ds(pl.multiple_of(g * MODES, MODES), MODES), :]

    block = MODES * TILE

    def swap_copy(source, target, n, where, phase):
        return pltpu.make_async_remote_copy(
            src_ref=source.at[pl.ds(pl.multiple_of(where, block), block), :],
            dst_ref=target.at[pl.ds(pl.multiple_of(n * block, block), block), :],
            send_sem=swap_sem.at[phase, 0, n],
            recv_sem=swap_sem.at[phase, 1, n],
            device_id=place(sibling),
            device_id_type=MESH,
        )

    def plane(d):
        return lax.rem(z + d, RING)

    def out_copy(n):
        return swap_copy(send, theirs, n, (other + n) * block, 0)

    def states(s, c):
        g = ordered(s)
        for n in range(4):
            load(g, n).wait()
        p = gated(ins[1, g], ins[2, g])
        r = gated(ins[3, g], ins[0, g])
        prod[g] = p
        grad[g] = r
        rates = group_rates(g)
        to_end = jnp.concatenate(split(jnp.exp(-rates * (span - 1.0 - lane))), axis=0)
        from_start = jnp.concatenate(split(jnp.exp(-rates * lane)), axis=0)
        ends = dot(to_end, p)
        starts = dot(from_start, r)
        ends = ends[:MODES] + ends[MODES:]
        starts = starts[:MODES] + starts[MODES:]
        for k in range(QUARTERS):
            cut = slice(k * LANES, (k + 1) * LANES)
            send[pl.ds(g * block + k, MODES, stride=TILE), :] = ends[:, cut]
            send[pl.ds(g * block + QUARTERS + k, MODES, stride=TILE), :] = starts[:, cut]
        return c

    for s in range(groups):
        states(s, 0)
    pl.semaphore_wait(barrier, chips)
    for d in FAR_PLANES:
        out_copy(plane(d)).start()

    sub = iota((TILE, LANES), 0)
    lead = (sub < QUARTERS) == (core == 0)

    def row_factor(n, width):
        rate = acol[pl.ds(first * MODES + n, 1), :]
        return jnp.broadcast_to(jnp.exp(-rate * float(span)), (width, LANES))

    def sweep(n, one):
        for m in range(MODES):
            one(n * MODES + m, 0)

    def tile_at(n):
        return pl.ds(pl.multiple_of(n * TILE, TILE), TILE)

    def own_tile(n):
        return pl.ds(pl.multiple_of(first * block + n * TILE, TILE), TILE)

    def combine(n, c):
        factor = row_factor(n, TILE)
        mine = send[own_tile(n), :]
        got = theirs[tile_at(n), :]
        comb[tile_at(n), :] = jnp.where(lead, factor, 1.0) * mine + jnp.where(lead, 1.0, factor) * got
        return c

    def message(source, target, t, send_sem, recv_sem):
        return pltpu.make_async_remote_copy(
            src_ref=source,
            dst_ref=target,
            send_sem=send_sem,
            recv_sem=recv_sem,
            device_id=place(t * 2 + core),
            device_id_type=MESH,
        )

    def await_all(part, sem):
        pltpu.make_async_copy(part, part, sem).wait()

    most = pl.ds(0, (chips - 1) * TILE)
    rest = pl.ds(0, chips - 1)
    for d in FAR_PLANES:
        n = plane(d)
        out_copy(n).wait_recv()
        sweep(n, combine)
        for shift, t in peers:
            if shift[0] == d:
                message(
                    comb.at[tile_at(t), :], recv.at[tile_at(chip), :], t, sems.at[0], sems.at[1]
                ).start()

    row = iota((span, LANES), 0)
    col = iota((span, LANES), 1)
    flip = (row + col == span - 1).astype(jnp.bfloat16)
    here = lane_i - iota((MODES, LANES), 0)

    xs[...] = jnp.zeros_like(xs)

    def within_chip(n, c):
        base = pl.multiple_of(first * block + n * TILE, TILE)
        near = pl.multiple_of(n * TILE, TILE)
        early = jnp.where(
            core == 0,
            send[pl.ds(base, QUARTERS), :] * theirs[pl.ds(near + QUARTERS, QUARTERS), :],
            theirs[pl.ds(near, QUARTERS), :] * send[pl.ds(base + QUARTERS, QUARTERS), :],
        )
        xs[pl.ds(first * MODES + n, 1), :] = jnp.sum(early, axis=0, keepdims=True)
        return c

    lax.fori_loop(0, part_rows, within_chip, 0, unroll=8)

    def pairs(g, total):
        pair = lax.dot_general(
            prod[g], grad[g], (((1,), (1,)), ((), ())), preferred_element_type=jnp.float32
        )
        hi, lo = split(pair)
        turned = dot(hi, flip) + dot(lo, flip)
        lagged = pltpu.roll(turned, 0, 1, stride=1, stride_axis=0)
        cross = jnp.sum(jnp.where(col >= row, lagged, 0.0), axis=0, keepdims=True)
        rates = group_rates(g)
        chip_part = xs[pl.ds(pl.multiple_of(g * MODES, MODES), MODES), :]
        inside = jnp.exp(-rates * (span - 1.0 - lane)) * cross + jnp.exp(-rates) * chip_part
        inside = jnp.sum(inside, axis=1, keepdims=True)
        return total + jnp.sum(jnp.where(here == g * MODES, inside, 0.0), axis=0, keepdims=True)

    share = lax.fori_loop(0, groups, pairs, jnp.zeros((1, LANES), jnp.float32), unroll=4)

    def reduce_start(level, buf, radix, stride, value):
        digit = lax.rem(lax.div(chip, stride), radix)
        base = chip - digit * stride
        vbuf[level] = value
        buf[digit] = value
        for d in range(1, radix):
            pltpu.make_async_remote_copy(
                src_ref=vbuf.at[level],
                dst_ref=buf.at[digit],
                send_sem=sems.at[4 + 2 * level],
                recv_sem=sems.at[5 + 2 * level],
                device_id=place((base + lax.rem(digit + d, radix) * stride) * 2 + core),
                device_id_type=MESH,
            ).start()

    def reduce_end(level, buf, radix):
        part = buf.at[pl.ds(0, radix - 1)]
        await_all(part, sems.at[5 + 2 * level])
        await_all(part, sems.at[4 + 2 * level])
        return jnp.sum(buf[...], axis=0)

    radix_one = 2 * RING
    radix_two = chips // radix_one
    reduce_start(0, v_one, radix_one, 1, share)

    turned_lags = jnp.where(lane_i == 0, 0, LANES - lane_i).astype(jnp.float32)
    triple = 3 * MODES
    token = iota((span, triple), 0).astype(jnp.float32)
    which = iota((span, triple), 1)

    def local(g, c):
        rates = group_rates(g)
        decay_row = small[0, pl.ds(g, 1), :]
        res_row = small[1, pl.ds(g, 1), :]
        weights = column(res_row)

        def toeplitz(lags, keep):
            line = jnp.sum(weights * jnp.exp(-rates * lags), axis=0, keepdims=True)
            full = pltpu.roll(jnp.broadcast_to(line, (span, LANES)), 0, 1, stride=1, stride_axis=0)
            return jnp.concatenate(split(jnp.where(keep, full, 0.0)), axis=1)

        p = prod[g]
        r = grad[g]
        mixed_ref[g] = dot(toeplitz(turned_lags, row >= col), jnp.concatenate([p, p], axis=0))
        conv_ref[g] = dot(toeplitz(lane, row <= col), jnp.concatenate([r, r], axis=0))
        decay_rows = jnp.concatenate([decay_row] * 3, axis=1)
        res_rows = jnp.concatenate([res_row] * 3, axis=1)

        def table(distance):
            hi, lo = split(res_rows * jnp.exp(-decay_rows * distance))
            return jnp.where(which < 2 * MODES, hi.astype(jnp.float32), lo.astype(jnp.float32)).astype(
                jnp.bfloat16
            )

        rise_ref[g] = table(token + 1.0)
        fall_ref[g] = table(span - token)
        return c

    lax.fori_loop(0, part_groups, local, 0, unroll=2)

    own = tile_at(chip)
    await_all(recv.at[most, :], sems.at[1])
    recv[own, :] = comb[own, :]

    rate = jnp.broadcast_to(acol[pl.ds(first * MODES + chip, 1), :], (QUARTERS, LANES))
    leap = jnp.exp(-rate * (2.0 * span))
    zero = jnp.zeros((QUARTERS, LANES), jnp.float32)

    def step(i, carry):
        rising, falling, acc = carry
        up = pl.multiple_of(i * TILE, TILE)
        down = pl.multiple_of((chips - 1 - i) * TILE, TILE)
        back[i, pl.ds(0, QUARTERS), :] = rising
        back[chips - 1 - i, pl.ds(QUARTERS, QUARTERS), :] = falling
        acc = acc + rising * recv[pl.ds(up + QUARTERS, QUARTERS), :]
        rising = leap * rising + recv[pl.ds(up, QUARTERS), :]
        falling = leap * falling + recv[pl.ds(down + QUARTERS, QUARTERS), :]
        return rising, falling, acc

    rising, falling, acc = lax.fori_loop(0, chips, step, (zero, zero, zero), unroll=8)
    pooled = jnp.sum(jnp.exp(-rate) * acc, axis=0, keepdims=True)
    for t in range(chips):
        back[t, TILE : TILE + 1, :] = pooled
    for d in FAR_PLANES:
        for shift, t in peers:
            if shift[0] == d:
                message(back.at[t], half.at[chip], t, sems.at[2], plane_sem.at[z]).start()
    half[chip] = back[chip]

    share = reduce_end(0, v_one, radix_one)
    reduce_start(1, v_two, radix_two, radix_one, share)
    lax.fori_loop(part_groups, groups, local, 0, unroll=2)

    def back_copy(n):
        return pltpu.make_async_remote_copy(
            src_ref=sib.at[pl.ds(pl.multiple_of(n * block, block), block), :],
            dst_ref=state_ref.at[pl.ds(pl.multiple_of((first + n) * block, block), block), :],
            send_sem=swap_sem.at[1, 0, n],
            recv_sem=swap_sem.at[1, 1, n],
            device_id=place(sibling),
            device_id_type=MESH,
        )

    def for_sibling(n, c):
        x = half[n, pl.ds(0, TILE), :]
        factor = row_factor(n, TILE)
        sib[tile_at(n), :] = jnp.where(lead, factor * x + send[own_tile(n), :], x)
        return c

    def for_me(n, c):
        x = half[n, pl.ds(0, TILE), :]
        factor = row_factor(n, TILE)
        state_ref[own_tile(n), :] = jnp.where(lead, x, factor * x + theirs[tile_at(n), :])
        return c

    sum_rows = here - first * MODES
    pooled_share = jnp.zeros((1, LANES), jnp.float32)
    for d in NEAR_PLANES:
        n = plane(d)
        count_in = MODES - 1 if d == 0 else MODES
        await_all(half.at[pl.ds(0, count_in)], plane_sem.at[n])
        sweep(n, for_sibling)
        back_copy(n).start()
        pools = jnp.concatenate(
            [half[n * MODES + m, TILE : TILE + 1, :] for m in range(MODES)], axis=0
        )
        pools = jnp.sum(pools, axis=1, keepdims=True)
        pooled_share = pooled_share + jnp.sum(
            jnp.where(sum_rows == n * MODES, pools, 0.0), axis=0, keepdims=True
        )
        if d != NEAR_PLANES[-1]:
            sweep(n, for_me)

    share = reduce_end(1, v_two, radix_two) + pooled_share
    vbuf[2] = share
    last = pltpu.make_async_remote_copy(
        src_ref=vbuf.at[2],
        dst_ref=v_got.at[0],
        send_sem=sems.at[8],
        recv_sem=sems.at[9],
        device_id=place(sibling),
        device_id_type=MESH,
    )
    last.start()
    n = plane(NEAR_PLANES[-1])
    sweep(n, for_me)
    last.wait()
    total_ref[...] = share + v_got[0]

    for n in range(part_groups):
        out_copy(n).wait_send()
        back_copy(n).wait()
    await_all(comb.at[most, :], sems.at[0])
    await_all(back.at[rest], sems.at[2])


def exchange(query_input, key_input, value_input, out_grad, residues, decays):
    inner = lax.axis_size("grp")
    count = lax.axis_size("ctx") * inner
    span, width = query_input.shape
    groups = width // GROUP
    rows = groups * MODES * TILE
    chips = count // 2
    f32 = jnp.float32
    bf16 = jnp.bfloat16

    def body(*refs):
        exchange_kernel(count, groups, span, inner, *refs)

    hbm = pl.BlockSpec(memory_space=pltpu.HBM)
    vmem = pl.BlockSpec(memory_space=pltpu.VMEM)
    return pl.pallas_call(
        body,
        out_shape=(
            jax.ShapeDtypeStruct((rows, LANES), f32),
            jax.ShapeDtypeStruct((1, LANES), f32),
            jax.ShapeDtypeStruct((4, groups, span, GROUP), bf16),
            jax.ShapeDtypeStruct((groups, span, GROUP), f32),
            jax.ShapeDtypeStruct((groups, span, GROUP), f32),
            jax.ShapeDtypeStruct((groups, span, 3 * MODES), bf16),
            jax.ShapeDtypeStruct((groups, span, 3 * MODES), bf16),
        ),
        in_specs=[hbm] * 6,
        out_specs=(vmem,) * 7,
        scratch_shapes=[
            pltpu.VMEM((groups, span, GROUP), bf16),
            pltpu.VMEM((groups, span, GROUP), bf16),
            pltpu.VMEM((rows, LANES), f32),
            pltpu.VMEM((rows // 2, LANES), f32),
            pltpu.VMEM((rows // 2, LANES), f32),
            pltpu.VMEM((chips * TILE, LANES), f32),
            pltpu.VMEM((chips, EXTRA, LANES), f32),
            pltpu.VMEM((chips, EXTRA, LANES), f32),
            pltpu.VMEM((rows // 2, LANES), f32),
            pltpu.VMEM((groups * MODES, LANES), f32),
            pltpu.VMEM((groups * MODES, LANES), f32),
            pltpu.VMEM((2, groups, MODES), f32),
            pltpu.VMEM((3, 1, LANES), f32),
            pltpu.VMEM((2 * RING, 1, LANES), f32),
            pltpu.VMEM((chips // (2 * RING), 1, LANES), f32),
            pltpu.VMEM((1, 1, LANES), f32),
            pltpu.SemaphoreType.DMA((groups, 4)),
            pltpu.SemaphoreType.DMA((2,)),
            pltpu.SemaphoreType.DMA((2, 2, groups // 2)),
            pltpu.SemaphoreType.DMA((RING,)),
            pltpu.SemaphoreType.DMA((10,)),
        ],
        compiler_params=pltpu.CompilerParams(
            collective_id=0, has_side_effects=True, vmem_limit_bytes=20 * MIB
        ),
    )(
        *(
            pltpu.with_memory_space_constraint(a, pltpu.HBM)
            for a in (query_input, key_input, value_input, out_grad, residues, decays)
        )
    )


def finish_kernel(
    groups, scale,
    state_ref, total_ref, ins, mixed_ref, conv_ref, rise_ref, fall_ref,
    out_hbm, qg_hbm, kg_hbm, vg_hbm, rg_hbm,
    outs, rg_ref, sems, rg_sem,
):
    targets = (out_hbm, qg_hbm, kg_hbm, vg_hbm)

    def store(g, n):
        return pltpu.make_async_copy(
            outs.at[n, g],
            targets[n].at[:, pl.ds(pl.multiple_of(g * GROUP, GROUP), GROUP)],
            sems.at[n, g],
        )

    def carried(table, g, offset):
        state = jnp.concatenate(
            [
                state_ref[pl.ds(g * MODES * TILE + offset + n, MODES, stride=TILE), :]
                for n in range(QUARTERS)
            ],
            axis=1,
        )
        hi, lo = split(state)
        return dot(table, jnp.concatenate([hi, lo, hi], axis=0))

    def one(g, c):
        mixed = mixed_ref[g] + carried(rise_ref[g], g, 0)
        outs[0, g] = ins[0, g].astype(jnp.float32) * mixed
        store(g, 0).start()
        outs[1, g] = ins[3, g].astype(jnp.float32) * mixed
        store(g, 1).start()
        conv = conv_ref[g] + carried(fall_ref[g], g, QUARTERS)
        outs[2, g] = ins[2, g].astype(jnp.float32) * conv
        store(g, 2).start()
        outs[3, g] = ins[1, g].astype(jnp.float32) * conv
        store(g, 3).start()
        return c

    for g in range(groups):
        one(g, 0)

    spread = jnp.broadcast_to(total_ref[...], (groups, LANES))
    own = lax.div(iota((groups, LANES), 1), MODES) == iota((groups, LANES), 0)
    spread = jnp.where(own, spread, 0.0)
    out = spread
    for n in range(1, groups):
        out = out + pltpu.roll(spread, LANES - n * MODES, 1)
    rg_ref[...] = out[:, :MODES] * scale
    small = pltpu.make_async_copy(rg_ref, rg_hbm, rg_sem)
    small.start()

    for g in range(groups):
        for n in range(4):
            store(g, n).wait()
    small.wait()


def finish(parts, span, width, length):
    groups = width // GROUP
    scale = 1.0 / (length * math.sqrt(GROUP))

    def body(*refs):
        finish_kernel(groups, scale, *refs)

    hbm = pl.BlockSpec(memory_space=pltpu.HBM)
    vmem = pl.BlockSpec(memory_space=pltpu.VMEM)
    big = jax.ShapeDtypeStruct((span, width), jnp.float32)
    return pl.pallas_call(
        body,
        out_shape=(big, big, big, big, jax.ShapeDtypeStruct((groups, MODES), jnp.float32)),
        in_specs=[vmem] * 7,
        out_specs=(hbm,) * 5,
        scratch_shapes=[
            pltpu.VMEM((4, groups, span, GROUP), jnp.float32),
            pltpu.VMEM((groups, MODES), jnp.float32),
            pltpu.SemaphoreType.DMA((4, groups)),
            pltpu.SemaphoreType.DMA(()),
        ],
        compiler_params=pltpu.CompilerParams(vmem_limit_bytes=20 * MIB),
    )(*parts)


def on_device(query_input, key_input, value_input, out_grad, residues, decay_rates):
    span, width = query_input.shape
    length = span * lax.axis_size("ctx") * lax.axis_size("grp")
    parts = exchange(query_input, key_input, value_input, out_grad, residues, decay_rates)
    return finish(parts, span, width, length)


def solution(mesh):
    rows = P(("ctx", "grp"), None)
    return jax.shard_map(
        on_device,
        mesh=mesh,
        in_specs=(rows, rows, rows, rows, P(), P()),
        out_specs=(rows, rows, rows, rows, P()),
        check_vma=False,
    )
```
